128 devices in a mesh: row: 8 (over x_hi, y), col: 16 (over z, x_lo, core).
Axes of the slice: x: 4 (x_hi: 2, x_lo: 2; x = x_hi * 2 + x_lo), y: 4, z: 4, core: 2. Of those that a mesh axis runs over, the one named last changes fastest.
Arguments:
- pair_ints: bfloat16 [2048, 16384], P(None, ('row', 'col')), may hold values from -0.59765625 to 0.59765625
- denominators: float32 [2048], replicated, may hold values from 0.5 to 4
- lap_points: float32 [3], replicated, may hold values from 0.05 to 1.5
- lap_weights: float32 [3], replicated, may hold values from 0.2 to 1
Outputs:
- aux_matrices: float32 [3, 16384, 16384], P(None, 'row', 'col')
The draws below stay inside these ranges and needn't reach their ends.
All inputs are finite; a program needn't handle non-finite values.
Results may differ from the reference program's by a relative error of at most 0.0027.
Values may be sent and summed in bfloat16 or wider, within the bound.
A program may use at most 128 MiB of HBM per device.

```python
import math
import jax
import jax.numpy as jnp
from jax import lax

NAUX = 16384
R = 2048
NT = 3


def block_scale(own_key, shape, shards, smallest, high):
    factor_of, own = 1.0, jax.random.fold_in(own_key, 6)
    for dim, blocks in shards:
        draws = jnp.exp(jax.random.uniform(jax.random.fold_in(own, dim), (blocks,), jnp.float32, smallest / len(shards), high / len(shards)))
        factor_of = factor_of * jnp.repeat(draws, shape[dim] // blocks).reshape([-1 if axis == dim else 1 for axis in range(len(shape))])
    return factor_of


def centred(key, extent, spread, reach, pieces=(), dtype=jnp.bfloat16):
    level = block_scale(key, extent, pieces, -0.22, 0.18) if pieces else 1.0
    entries = jax.random.normal(key, extent, jnp.float32) * spread * level
    return jnp.minimum(jnp.maximum(entries, -reach), reach).astype(dtype)


def setup_inputs(seed: int = 0) -> dict:
    streams_of = jax.random.split(jax.random.key(seed), 5)
    pair_ints = centred(streams_of[0], (R, NAUX), 0.08, 0.59765625, ((1, 128),))
    denominators = jnp.clip(jax.random.uniform(streams_of[1], (R,), jnp.float32, 0.5, 4.0), 0.5, 4.0)
    lap_points = jnp.clip(jnp.exp(jax.random.uniform(streams_of[2], (NT,), jnp.float32, math.log(0.05), math.log(1.5))), 0.05, 1.5)
    lap_weights = jnp.clip(jnp.exp(jax.random.uniform(streams_of[3], (NT,), jnp.float32, math.log(0.2), math.log(1.0))), 0.2, 1.0)
    return {"pair_ints": pair_ints, "denominators": denominators, "lap_points": lap_points, "lap_weights": lap_weights}


def reference(pair_ints, denominators, lap_points, lap_weights):
    values = pair_ints.astype(jnp.float32)

    def single(inputs):
        point, weight = inputs
        factor = weight * jnp.exp(-point * denominators)
        weighted = (values * factor[:, None]).astype(jnp.bfloat16)
        weighted = lax.optimization_barrier(weighted).astype(jnp.float32)
        return jnp.dot(weighted.T, values, precision=lax.Precision.HIGHEST)

    return lax.map(single, (lap_points, lap_weights))
```

```python
import jax
import jax.numpy as jnp
from jax import lax
from jax.experimental import pallas as pl
from jax.experimental.pallas import tpu as pltpu
from jax.sharding import PartitionSpec as P

NC, NG, SMAX, NT, NE = 8, 4, 5, 6, 27
TARGETS = ((0, 12), (0, 4), (4, 2), (0, 1), (0, 2), (1, 1), (3, 0), (3, 1), (1, 0), (4, 3))
PROGRAMS = (
    (
        (
            (0, 0, -1, 0, 0, ((0, 0, 0, 2), (1, 0, 0, 5), (2, 2, 0, 1), (3, 0, 0, 0)), 1),
            (0, 1, 0, 0, 1, (), 1),
            (0, 2, 1, 2, 0, ((1, 2, 1, 8),), 0),
            (0, 2, 2, 2, 1, ((2, 1, 1, 9), (4, 1, 1, 7)), 0),
            (0, 3, 3, 0, 12, ((5, 1, 12, 8), (1, 0, 12, 10), (3, 0, 12, 4)), 0),
            (0, 3, 4, 0, 2, ((1, 0, 2, 13), (3, 0, 2, 5)), 1),
            (0, 3, 5, 0, 4, ((6, 1, 4, 10), (4, 0, 4, 12), (0, 0, 4, 8), (3, 0, 4, 6)), 1),
            (1, 0, 7, 0, 3, (), 1),
            (1, 0, 8, 0, 5, (), 1),
            (1, 1, 9, 0, 14, ((5, 1, 14, 11), (3, 0, 14, 10)), 0),
            (1, 1, 10, 2, 2, ((2, 1, 5, 19), (4, 1, 5, 16)), 0),
            (1, 2, 11, 0, 6, ((3, 0, 6, 11),), 1),
            (1, 2, 12, 0, 8, ((3, 0, 8, 12),), 0),
            (1, 2, 14, 2, 3, ((2, 1, 4, 20), (4, 1, 4, 17)), 0),
            (1, 3, 15, 0, 7, (), 1),
            (2, 0, 17, 2, 4, ((4, 1, 0, 21),), 0),
            (2, 3, 19, 0, 10, ((7, 1, 10, 23), (3, 0, 10, 16)), 0),
            (3, 0, 20, 2, 5, ((2, 1, 3, 23),), 0),
        ),
        ((6, 0, 13), (13, 0, 15), (16, 0, 9), (18, 0, 11)),
    ),
    (
        (
            (0, 0, -1, 0, 1, ((0, 0, 1, 1), (1, 0, 1, 3), (5, 1, 1, 1), (3, 0, 1, 0)), 0),
            (0, 2, 1, 0, 13, ((4, 0, 13, 5), (3, 0, 13, 6)), 1),
            (0, 2, 2, 0, 3, ((1, 0, 3, 9), (0, 0, 3, 7), (7, 1, 3, 7), (3, 0, 3, 7)), 0),
            (0, 2, 3, 0, 5, ((5, 1, 5, 6), (7, 1, 5, 8), (3, 0, 5, 8)), 0),
            (1, 0, 4, 0, 12, (), 1),
            (1, 1, 7, 0, 15, ((6, 1, 15, 15), (0, 0, 15, 13), (3, 0, 15, 13)), 1),
            (1, 2, 8, 0, 9, ((8, 1, 9, 14), (3, 0, 9, 16)), 1),
            (1, 2, 9, 0, 7, ((3, 0, 7, 15),), 0),
            (1, 2, 10, 0, 14, (), 1),
            (1, 3, 12, 0, 8, (), 1),
            (2, 0, 13, 0, 11, ((6, 1, 11, 20), (8, 1, 11, 19), (3, 0, 11, 18)), 1),
            (2, 0, 14, 2, 0, ((0, 2, 2, 19),), 0),
            (2, 1, 15, 2, 1, ((2, 1, 14, 17),), 0),
            (3, 0, 16, 0, 10, (), 1),
        ),
        ((0, 0, 0), (5, 0, 2), (6, 0, 4), (11, 0, 6)),
    ),
    (
        (
            (0, 0, -1, 0, 2, ((2, 1, 2, 4), (4, 0, 2, 4), (0, 0, 2, 1), (1, 0, 2, 2), (3, 0, 2, 0)), 0),
            (0, 3, 2, 0, 14, ((9, 1, 14, 10), (1, 0, 14, 9), (3, 0, 14, 3)), 0),
            (0, 3, 3, 0, 6, ((8, 2, 3, 14), (3, 0, 6, 4)), 0),
            (1, 1, 6, 1, 7, ((6, 1, 7, 16),), 0),
            (1, 1, 7, 1, 1, ((6, 1, 1, 18),), 0),
            (1, 2, 8, 0, 12, ((5, 2, 1, 15), (3, 0, 12, 10)), 0),
            (1, 2, 9, 2, 0, ((1, 1, 7, 17),), 0),
            (1, 3, 12, 0, 4, ((0, 0, 4, 15), (2, 1, 4, 18), (3, 0, 4, 12)), 0),
            (1, 3, 14, 0, 10, ((4, 0, 10, 19), (3, 0, 10, 16)), 0),
            (2, 2, 18, 0, 8, ((9, 1, 8, 23), (3, 0, 8, 18)), 0),
            (2, 3, 22, 0, 0, ((3, 0, 0, 22),), 0),
        ),
        ((0, 0, 3), (1, 1, 3), (4, 0, 15), (5, 0, 7), (10, 0, 13), (11, 0, 11), (13, 0, 5), (15, 1, 2), (16, 1, 5), (17, 1, 4), (19, 0, 9), (20, 0, 1), (21, 1, 0), (23, 1, 6)),
    ),
    (
        (
            (0, 0, -1, 0, 3, ((0, 0, 3, 1), (1, 0, 3, 2), (5, 2, 1, 2), (4, 0, 3, 2), (3, 0, 3, 0)), 0),
            (0, 2, 1, 0, 15, ((4, 0, 15, 7), (1, 0, 15, 8), (3, 0, 15, 4)), 0),
            (0, 3, 2, 0, 7, ((5, 2, 2, 10), (4, 0, 7, 9), (3, 0, 7, 5)), 0),
            (1, 1, 5, 0, 13, ((3, 0, 13, 10),), 0),
            (1, 1, 6, 0, 11, ((2, 1, 11, 16), (3, 0, 11, 11)), 0),
            (1, 2, 7, 0, 5, ((9, 1, 5, 15), (0, 0, 5, 14), (3, 0, 5, 13)), 0),
            (1, 2, 8, 1, 14, ((6, 1, 14, 16),), 0),
            (1, 3, 9, 2, 0, ((1, 1, 14, 17),), 0),
            (2, 0, 11, 1, 12, ((6, 1, 12, 18),), 0),
            (2, 0, 13, 2, 1, ((0, 1, 12, 16),), 0),
            (2, 0, 14, 1, 11, ((6, 1, 11, 19),), 0),
            (2, 1, 15, 0, 9, ((3, 0, 9, 19),), 0),
            (2, 1, 17, 0, 1, ((7, 2, 3, 21), (5, 2, 5, 20), (3, 0, 1, 20)), 0),
            (3, 0, 21, 2, 2, ((0, 1, 15, 23),), 0),
        ),
        ((0, 0, 2), (3, 0, 14), (4, 0, 6), (10, 0, 12), (12, 0, 4), (16, 0, 10), (18, 0, 8), (19, 1, 9), (20, 1, 15), (22, 0, 0), (23, 1, 13), (24, 1, 10), (25, 1, 8)),
    ),
    (
        (
            (0, 0, -1, 0, 4, ((1, 0, 4, 5), (0, 0, 4, 1), (4, 0, 4, 3), (3, 0, 4, 0)), 0),
            (0, 2, 1, 2, 0, ((0, 1, 6, 8),), 0),
            (0, 3, 2, 0, 6, ((1, 0, 6, 11), (3, 0, 6, 4)), 0),
            (0, 3, 3, 0, 8, ((4, 0, 8, 12), (7, 2, 0, 9), (1, 0, 8, 12), (3, 0, 8, 5)), 0),
            (1, 0, 5, 0, 0, ((4, 0, 0, 15), (0, 0, 0, 15), (3, 0, 0, 7)), 0),
            (1, 1, 8, 2, 1, ((2, 1, 1, 12),), 0),
            (1, 1, 9, 2, 2, ((0, 1, 4, 17),), 0),
            (1, 2, 10, 0, 12, ((3, 0, 12, 10),), 0),
            (1, 3, 12, 0, 10, ((3, 0, 10, 15),), 0),
            (1, 3, 13, 0, 2, ((0, 0, 2, 20), (3, 0, 2, 14)), 0),
            (2, 0, 17, 0, 14, ((3, 0, 14, 17),), 0),
            (2, 1, 19, 1, 0, ((2, 2, 1, 20),), 0),
            (3, 0, 21, 2, 3, ((2, 1, 7, 22), (8, 2, 0, 20)), 0),
            (3, 3, 22, 1, 6, ((8, 1, 6, 24),), 0),
        ),
        ((0, 0, 5), (4, 0, 7), (6, 0, 9), (7, 0, 1), (11, 0, 13), (14, 0, 3), (15, 0, 11), (16, 1, 1), (18, 1, 7), (20, 0, 15), (23, 1, 3), (24, 1, 2), (25, 1, 5), (26, 1, 4)),
    ),
    (
        (
            (0, 0, -1, 0, 5, ((4, 0, 5, 3), (1, 0, 5, 3), (0, 0, 5, 1), (3, 0, 5, 0)), 0),
            (0, 2, 1, 0, 7, ((3, 0, 7, 4),), 0),
            (0, 2, 2, 0, 9, ((4, 0, 9, 9), (3, 0, 9, 6)), 0),
            (0, 3, 3, 0, 1, ((7, 2, 0, 9), (4, 0, 1, 11), (3, 0, 1, 7)), 0),
            (1, 1, 6, 0, 13, ((3, 0, 13, 11),), 0),
            (1, 1, 8, 0, 11, ((3, 0, 11, 15),), 0),
            (1, 1, 9, 0, 3, ((3, 0, 3, 14),), 0),
            (2, 0, 11, 1, 9, ((6, 1, 9, 20),), 0),
            (2, 0, 12, 2, 0, ((8, 2, 1, 19), (2, 1, 11, 18)), 0),
            (2, 0, 13, 0, 15, ((3, 0, 15, 20),), 0),
            (2, 1, 16, 1, 8, ((2, 2, 0, 20), (8, 1, 8, 21)), 0),
            (2, 3, 18, 1, 10, ((8, 1, 10, 22),), 0),
            (2, 3, 19, 1, 13, ((8, 1, 13, 24),), 0),
            (2, 3, 20, 1, 11, ((6, 1, 11, 23),), 0),
            (3, 1, 21, 1, 12, ((6, 1, 12, 24),), 0),
            (4, 1, 23, 1, 14, ((6, 1, 14, 25),), 0),
        ),
        ((0, 0, 4), (4, 0, 6), (5, 0, 8), (7, 0, 0), (10, 0, 12), (14, 0, 2), (15, 0, 10), (17, 0, 14), (22, 1, 15)),
    ),
    (
        (
            (0, 0, -1, 0, 6, ((1, 0, 6, 3), (0, 0, 6, 3), (4, 0, 6, 2), (3, 0, 6, 0)), 0),
            (0, 3, 1, 0, 10, ((9, 2, 0, 6), (3, 0, 10, 4)), 0),
            (0, 3, 2, 0, 2, ((3, 0, 2, 6),), 0),
            (0, 3, 3, 0, 4, ((3, 0, 4, 5),), 0),
            (1, 2, 9, 0, 14, ((3, 0, 14, 12),), 0),
            (1, 2, 10, 1, 2, ((8, 1, 2, 19), (2, 2, 0, 15)), 0),
            (1, 3, 12, 0, 8, ((1, 0, 8, 18), (3, 0, 8, 13)), 0),
            (2, 0, 15, 0, 0, ((0, 0, 0, 16), (1, 0, 0, 22), (3, 0, 0, 16)), 0),
            (2, 1, 16, 0, 12, ((3, 0, 12, 18),), 0),
            (3, 3, 20, 2, 0, ((2, 1, 5, 24), (4, 1, 5, 25)), 0),
            (3, 3, 22, 2, 1, ((4, 1, 2, 24),), 0),
        ),
        ((0, 0, 7), (4, 0, 11), (5, 0, 5), (6, 0, 3), (7, 1, 5), (8, 1, 3), (11, 0, 15), (13, 0, 9), (14, 0, 1), (17, 1, 7), (18, 0, 13), (19, 1, 1), (21, 1, 6), (23, 1, 0), (24, 1, 4)),
    ),
    (
        (
            (0, 0, -1, 0, 7, ((7, 2, 0, 1), (1, 0, 7, 2), (0, 0, 7, 5), (4, 0, 7, 1), (3, 0, 7, 0)), 0),
            (0, 2, 1, 0, 11, ((1, 0, 11, 6), (3, 0, 11, 4)), 0),
            (0, 3, 2, 0, 3, ((0, 0, 3, 13), (3, 0, 3, 6)), 0),
            (0, 3, 3, 0, 5, ((1, 0, 5, 7), (0, 0, 5, 11), (3, 0, 5, 5)), 0),
            (1, 1, 7, 1, 11, ((4, 2, 0, 12), (8, 1, 11, 11)), 0),
            (1, 1, 8, 0, 15, ((4, 0, 15, 13), (3, 0, 15, 11)), 0),
            (1, 1, 9, 0, 9, ((2, 2, 1, 13), (3, 0, 9, 13)), 0),
            (1, 2, 10, 2, 0, ((6, 2, 0, 14),), 0),
            (1, 2, 11, 0, 1, ((3, 0, 1, 14),), 0),
            (2, 0, 14, 0, 13, ((3, 0, 13, 18),), 0),
            (2, 0, 15, 1, 9, ((8, 1, 9, 20),), 0),
            (2, 2, 17, 1, 14, ((8, 1, 14, 21),), 0),
            (2, 3, 19, 2, 1, ((2, 1, 9, 20),), 0),
            (2, 3, 20, 1, 13, ((8, 1, 13, 22),), 0),
            (3, 2, 23, 1, 12, ((8, 1, 12, 23),), 0),
        ),
        ((0, 0, 6), (4, 0, 10), (5, 0, 4), (6, 0, 2), (12, 0, 14), (13, 0, 8), (16, 0, 0), (18, 0, 12), (21, 1, 10), (22, 1, 8), (24, 1, 15)),
    ),
    (
        (
            (0, 0, -1, 0, 8, ((0, 0, 8, 3), (4, 0, 8, 1), (1, 0, 8, 3), (3, 0, 8, 0)), 0),
            (0, 3, 1, 0, 4, ((4, 0, 4, 7), (3, 0, 4, 5)), 0),
            (0, 3, 2, 0, 12, ((3, 0, 12, 6),), 0),
            (0, 3, 3, 0, 10, ((1, 0, 10, 11), (0, 0, 10, 12), (3, 0, 10, 7)), 0),
            (1, 1, 7, 2, 0, ((2, 2, 1, 13),), 0),
            (1, 1, 8, 1, 6, ((8, 1, 6, 13), (6, 1, 6, 13)), 0),
            (1, 2, 9, 0, 14, ((0, 0, 14, 17), (3, 0, 14, 12)), 0),
            (1, 2, 10, 1, 7, ((6, 1, 7, 14), (8, 1, 7, 14)), 0),
            (1, 3, 12, 0, 6, ((1, 0, 6, 16), (3, 0, 6, 14)), 0),
            (1, 3, 15, 0, 0, ((3, 0, 0, 16),), 0),
            (2, 0, 16, 1, 2, ((6, 1, 2, 17),), 0),
            (2, 1, 18, 1, 3, ((6, 1, 3, 19),), 0),
            (2, 1, 19, 2, 1, ((2, 2, 2, 21),), 0),
            (2, 2, 20, 0, 2, ((3, 0, 2, 20),), 0),
            (3, 0, 22, 1, 0, ((8, 1, 0, 19), (6, 1, 0, 21)), 0),
            (3, 0, 23, 1, 1, ((8, 1, 1, 20), (6, 1, 1, 22)), 0),
        ),
        ((0, 0, 9), (4, 0, 5), (5, 0, 13), (6, 0, 11), (11, 0, 15), (13, 0, 7), (14, 0, 1), (17, 1, 4), (21, 0, 3), (24, 1, 5)),
    ),
    (
        (
            (0, 0, -1, 0, 9, ((0, 0, 9, 2), (1, 0, 9, 2), (4, 0, 9, 2), (3, 0, 9, 0)), 0),
            (0, 2, 1, 0, 5, ((1, 0, 5, 6), (3, 0, 5, 4)), 0),
            (0, 2, 2, 0, 13, ((4, 0, 13, 10), (0, 0, 13, 6), (3, 0, 13, 5)), 0),
            (0, 3, 3, 0, 11, ((1, 0, 11, 8), (0, 0, 11, 8), (3, 0, 11, 6)), 0),
            (0, 3, 4, 1, 11, ((8, 1, 11, 12),), 0),
            (1, 1, 8, 2, 0, ((2, 1, 11, 15), (4, 1, 11, 17)), 0),
            (1, 1, 9, 0, 15, ((3, 0, 15, 11),), 0),
            (1, 1, 10, 0, 7, ((3, 0, 7, 13),), 0),
            (1, 1, 11, 0, 1, ((3, 0, 1, 14),), 0),
            (2, 1, 15, 1, 12, ((8, 1, 12, 21),), 0),
            (2, 1, 17, 0, 3, ((3, 0, 3, 21),), 0),
            (3, 3, 22, 2, 1, ((2, 1, 15, 23),), 0),
        ),
        ((0, 0, 8), (5, 0, 4), (6, 0, 12), (7, 0, 10), (12, 0, 14), (13, 1, 10), (14, 0, 6), (16, 0, 0), (18, 1, 13), (19, 1, 14), (20, 0, 2), (21, 1, 15), (23, 1, 8), (24, 1, 9)),
    ),
    (
        (
            (0, 0, -1, 0, 10, ((0, 0, 10, 1), (1, 0, 10, 3), (4, 0, 10, 3), (3, 0, 10, 0)), 0),
            (0, 3, 1, 0, 8, ((1, 0, 8, 7), (3, 0, 8, 6)), 0),
            (0, 3, 2, 0, 14, ((3, 0, 14, 7),), 0),
            (0, 3, 3, 0, 6, ((4, 0, 6, 12), (1, 0, 6, 12), (3, 0, 6, 8)), 0),
            (1, 2, 7, 0, 4, ((3, 0, 4, 14),), 0),
            (1, 2, 8, 0, 12, ((0, 0, 12, 16), (3, 0, 12, 15)), 0),
            (1, 2, 9, 0, 2, ((3, 0, 2, 16),), 0),
            (2, 0, 13, 1, 4, ((6, 1, 4, 17),), 0),
            (2, 3, 16, 0, 0, ((3, 0, 0, 22),), 0),
            (3, 0, 17, 1, 7, ((8, 1, 7, 24),), 0),
            (3, 1, 18, 2, 0, ((0, 1, 0, 23),), 0),
            (3, 3, 19, 1, 2, ((6, 1, 2, 23),), 0),
            (3, 3, 20, 1, 3, ((6, 1, 3, 24),), 0),
        ),
        ((0, 0, 11), (4, 0, 9), (5, 0, 15), (6, 0, 7), (10, 0, 13), (11, 0, 5), (12, 0, 3), (14, 1, 5), (15, 0, 1), (21, 1, 6), (22, 1, 0), (23, 1, 1)),
    ),
    (
        (
            (0, 0, -1, 0, 11, ((0, 0, 11, 1), (4, 0, 11, 3), (1, 0, 11, 3), (3, 0, 11, 0)), 0),
            (0, 2, 1, 2, 0, ((8, 2, 0, 8),), 0),
            (0, 2, 2, 0, 9, ((1, 0, 9, 6), (3, 0, 9, 4)), 0),
            (0, 2, 3, 2, 1, ((0, 1, 11, 7),), 0),
            (0, 2, 4, 0, 15, ((4, 0, 15, 9), (3, 0, 15, 5)), 0),
            (0, 2, 5, 0, 7, ((1, 0, 7, 9), (4, 0, 7, 10), (3, 0, 7, 6)), 0),
            (1, 1, 9, 1, 8, ((8, 1, 8, 13),), 0),
            (1, 1, 10, 0, 13, ((0, 0, 13, 14), (3, 0, 13, 10)), 0),
            (1, 1, 11, 0, 5, ((3, 0, 5, 11),), 0),
            (1, 1, 12, 1, 9, ((6, 1, 9, 12), (2, 2, 4, 17)), 0),
            (1, 2, 13, 0, 3, ((4, 0, 3, 17), (3, 0, 3, 12)), 0),
            (2, 0, 18, 0, 1, ((3, 0, 1, 15),), 0),
            (2, 0, 19, 1, 12, ((8, 1, 12, 19),), 0),
            (2, 1, 20, 1, 13, ((6, 1, 13, 20), (8, 1, 13, 21)), 0),
            (3, 0, 21, 1, 14, ((6, 1, 14, 22),), 0),
        ),
        ((0, 0, 10), (6, 0, 8), (7, 0, 14), (8, 0, 6), (14, 0, 4), (15, 0, 12), (16, 0, 2), (17, 1, 11), (22, 0, 0), (23, 1, 10), (24, 1, 15)),
    ),
    (
        (
            (0, 0, -1, 0, 12, ((0, 0, 12, 3), (4, 0, 12, 2), (1, 0, 12, 2), (3, 0, 12, 0)), 0),
            (0, 2, 1, 0, 14, ((0, 0, 14, 9), (1, 0, 14, 9), (3, 0, 14, 3)), 0),
            (0, 3, 2, 0, 0, ((4, 0, 0, 9), (2, 2, 0, 10), (3, 0, 0, 4)), 0),
            (0, 3, 3, 0, 8, ((3, 0, 8, 5),), 0),
            (1, 2, 6, 2, 0, ((1, 1, 3, 18),), 0),
            (1, 2, 7, 0, 2, ((3, 0, 2, 9),), 0),
            (1, 2, 8, 0, 4, ((3, 0, 4, 10),), 0),
            (1, 3, 11, 0, 10, ((3, 0, 10, 11),), 0),
            (2, 0, 13, 2, 1, ((1, 1, 0, 22),), 0),
            (2, 2, 16, 0, 6, ((6, 2, 0, 18), (3, 0, 6, 18)), 0),
            (3, 2, 19, 1, 6, ((6, 1, 6, 22),), 0),
            (3, 2, 20, 1, 0, ((6, 1, 0, 21),), 0),
            (3, 3, 21, 1, 7, ((6, 1, 7, 23),), 0),
            (4, 0, 22, 1, 1, ((8, 1, 1, 23),), 0),
        ),
        ((0, 0, 13), (4, 0, 1), (5, 0, 9), (9, 0, 5), (10, 0, 3), (12, 0, 11), (14, 0, 15), (15, 0, 7), (17, 1, 2), (18, 1, 3), (23, 1, 4), (24, 1, 5)),
    ),
    (
        (
            (0, 0, -1, 0, 13, ((6, 2, 1, 3), (1, 0, 13, 2), (4, 0, 13, 2), (0, 0, 13, 1), (3, 0, 13, 0)), 0),
            (0, 2, 1, 0, 1, ((4, 0, 1, 8), (1, 0, 1, 11), (3, 0, 1, 4)), 0),
            (0, 3, 2, 0, 9, ((0, 0, 9, 8), (3, 0, 9, 5)), 0),
            (1, 1, 6, 0, 5, ((3, 0, 5, 9),), 0),
            (1, 1, 7, 0, 3, ((3, 0, 3, 10),), 0),
            (1, 2, 8, 0, 11, ((0, 0, 11, 13), (3, 0, 11, 12)), 0),
            (2, 0, 12, 1, 15, ((4, 2, 0, 18), (8, 1, 15, 17)), 0),
            (2, 1, 13, 0, 15, ((3, 0, 15, 14),), 0),
            (2, 1, 14, 0, 7, ((3, 0, 7, 15),), 0),
            (2, 1, 15, 2, 0, ((4, 1, 11, 19),), 0),
            (2, 3, 16, 2, 1, ((8, 2, 2, 21), (2, 1, 8, 19)), 0),
            (3, 0, 19, 2, 2, ((8, 2, 3, 24), (2, 1, 15, 21)), 0),
            (3, 0, 20, 1, 11, ((2, 2, 1, 22), (8, 1, 11, 25)), 0),
            (3, 3, 22, 1, 8, ((8, 1, 8, 26),), 0),
            (3, 3, 23, 1, 9, ((6, 1, 9, 24),), 0),
        ),
        ((0, 0, 12), (3, 0, 14), (4, 0, 0), (5, 0, 8), (9, 0, 2), (10, 0, 4), (11, 0, 10), (17, 1, 10), (18, 0, 6), (21, 1, 14), (24, 1, 12), (25, 1, 13)),
    ),
    (
        (
            (0, 0, -1, 0, 14, ((4, 0, 14, 1), (0, 0, 14, 2), (1, 0, 14, 2), (3, 0, 14, 0)), 0),
            (0, 3, 1, 0, 2, ((1, 0, 2, 9), (4, 0, 2, 7), (3, 0, 2, 5)), 0),
            (0, 3, 2, 0, 12, ((0, 0, 12, 8), (1, 0, 12, 8), (3, 0, 12, 4)), 0),
            (1, 0, 3, 0, 10, ((0, 0, 10, 14), (3, 0, 10, 7)), 0),
            (1, 2, 7, 0, 8, ((3, 0, 8, 10),), 0),
            (1, 2, 9, 0, 0, ((6, 2, 1, 19), (3, 0, 0, 11)), 0),
            (1, 3, 12, 0, 6, ((3, 0, 6, 13),), 0),
            (2, 1, 14, 1, 1, ((8, 1, 1, 18),), 0),
            (2, 2, 15, 0, 4, ((3, 0, 4, 15),), 0),
            (2, 3, 17, 1, 4, ((8, 1, 4, 19),), 0),
            (3, 0, 19, 1, 5, ((8, 1, 5, 21),), 0),
            (3, 1, 20, 2, 0, ((4, 1, 1, 22),), 0),
        ),
        ((0, 0, 15), (4, 0, 13), (5, 0, 3), (6, 0, 11), (8, 0, 9), (10, 0, 1), (11, 0, 7), (13, 1, 0), (16, 0, 5), (18, 1, 2), (21, 1, 6), (22, 1, 7), (23, 1, 3)),
    ),
    (
        (
            (0, 0, -1, 0, 15, ((0, 0, 15, 1), (2, 2, 0, 1), (1, 0, 15, 4), (3, 0, 15, 0)), 0),
            (0, 2, 1, 0, 3, ((7, 2, 0, 7), (3, 0, 3, 5)), 0),
            (0, 2, 2, 0, 13, ((2, 2, 2, 9), (3, 0, 13, 4)), 0),
            (0, 3, 3, 0, 11, ((3, 0, 11, 6),), 0),
            (1, 1, 6, 0, 9, ((0, 0, 9, 15), (3, 0, 9, 8)), 0),
            (1, 1, 8, 0, 1, ((0, 0, 1, 17), (1, 0, 1, 18), (3, 0, 1, 10)), 0),
            (1, 2, 9, 0, 7, ((4, 0, 7, 14), (3, 0, 7, 11)), 0),
            (2, 0, 12, 1, 8, ((4, 2, 1, 16), (8, 1, 8, 17)), 0),
            (2, 1, 14, 0, 5, ((3, 0, 5, 16),), 0),
            (3, 0, 16, 1, 12, ((8, 1, 12, 21),), 0),
            (3, 0, 18, 2, 0, ((2, 1, 15, 22),), 0),
            (3, 0, 20, 2, 1, ((6, 2, 1, 22), (4, 1, 9, 23)), 0),
            (3, 2, 21, 2, 2, ((2, 1, 10, 23),), 0),
            (3, 3, 22, 1, 14, ((6, 1, 14, 23),), 0),
            (3, 3, 23, 1, 15, ((6, 1, 15, 24), (8, 1, 15, 25)), 0),
            (3, 3, 24, 2, 3, ((2, 1, 13, 26),), 0),
        ),
        ((0, 0, 14), (4, 0, 12), (5, 0, 2), (7, 0, 10), (10, 0, 8), (11, 0, 0), (13, 0, 6), (15, 0, 4), (17, 1, 13), (19, 1, 11), (25, 1, 9), (26, 1, 10)),
    ),
)
VMEM_LIMIT = 24 << 20

F32, BF16 = jnp.float32, jnp.bfloat16
MESH = pl.DeviceIdType.MESH
NT_PTS = 3
PAIRS, ROWS, COLS, OWN = 2048, 2048, 1024, 128
KC = PAIRS // NC
KK = 512
NK = PAIRS // KK
PER = KK // KC
MB, NB = 256, 256
NM = ROWS // MB
START = SMAX + PER
STEPS = NC + SMAX


def flip(value, bits):
    return [jnp.int32(b) * (1 - 2 * ((value // b) % 2)) for b in bits]


def flipped(value, deltas, bits, mask):
    for delta, bit in zip(deltas, bits):
        if mask & bit:
            value = value + delta
    return value


def weigh(x, factor, w_ref):
    x = x.astype(F32)
    for t in range(NT_PTS):
        w_ref[pl.ds(t * MB, MB), :] = (x * factor(t)).astype(BF16)


def product(w, y):
    return lax.dot_general(w, y, (((1,), (1,)), ((), ())), preferred_element_type=F32)


def gather_kernel(points, weights, own_ref, den_ref, acc, x_ref, y_ref, f_ref,
                  transit, w_ref, send_sem, recv_sem, local_sem):
    row, col = lax.axis_index("row"), lax.axis_index("col")
    row_d, col_d = flip(row, (1, 2, 4)), flip(col, (1, 2, 4, 8))
    peers = [
        {"row": flipped(row, row_d, (1, 2, 4), dr), "col": flipped(col, col_d, (1, 2, 4, 8), dc)}
        for dr, dc in TARGETS
    ]
    barrier = pltpu.get_barrier_semaphore()
    for peer in peers:
        pl.semaphore_signal(barrier, inc=1, device_id=peer, device_id_type=MESH)

    high = row // 4
    code = row * 2 + high
    code_d = flip(code, (1, 2, 4, 8))

    def lanes(j):
        return pl.ds(pl.multiple_of((j % PER) * KC, KC), KC)

    def place(kind, mark, j):
        if kind == 2:
            return transit.at[j, mark]
        slot = flipped(code, code_d, (1, 2, 4, 8), mark)
        if kind == 0:
            return x_ref.at[j // PER, pl.ds(pl.multiple_of(slot * OWN, OWN), OWN), lanes(j)]
        slot = slot % 8
        return y_ref.at[j // PER, pl.ds(pl.multiple_of(slot * OWN, OWN), OWN), lanes(j)]

    for k in range(NK):
        x_ref[k, pl.ds(pl.multiple_of(col * OWN, OWN), OWN), :] = own_ref[pl.ds(k * KK, KK), :].T
    for t in range(NT_PTS):
        f_ref[t] = weights[t] * jnp.exp(-points[t] * den_ref[...])
    pl.semaphore_wait(barrier, len(TARGETS))

    k_col = col // 2
    bits = [((row // b) % 2 + (k_col // b) % 2) % 2 for b in (4, 2, 1)]
    which = (bits[0] * 4 + bits[1] * 2 + bits[2]) * 2 + ((col % 2) + high) % 2

    def arrived(kind, mark, event, j):
        ref = place(kind, mark, j)
        pltpu.make_async_copy(ref, ref, recv_sem.at[j, event]).wait()

    def act(action, j):
        _, _, event, kind, mark, kids, local = action
        if event >= 0:
            arrived(kind, mark, event, j)
        src = place(kind, mark, j)
        for target, to_kind, to_mark, to_event in kids:
            pltpu.make_async_remote_copy(
                src_ref=src, dst_ref=place(to_kind, to_mark, j),
                send_sem=send_sem.at[j], recv_sem=recv_sem.at[j, to_event],
                device_id=peers[target], device_id_type=MESH,
            ).start()
        if local:
            pltpu.make_async_copy(src, place(1, mark, j), local_sem.at[j]).start()

    def bulk_wait(sem, copies):
        ref = acc.at[0, pl.ds(0, copies * OWN * KC // (2 * COLS)), :]
        pltpu.make_async_copy(ref, ref, sem).wait()

    def settle(j):
        for g, (actions, last) in enumerate(PROGRAMS):
            @pl.when(which == g)
            def _():
                for event, kind, mark in last:
                    arrived(kind, mark, event, j)
                copies = sum(a[6] for a in actions)
                if copies:
                    bulk_wait(local_sem.at[j], copies)

    def block(k, m, first):
        rows = pl.ds(pl.multiple_of(m * MB, MB), MB)
        weigh(x_ref[k, rows, :], lambda t: f_ref[t, pl.ds(k, 1), :], w_ref)

        @pl.loop(0, COLS // NB)
        def _(n):
            at = pl.ds(pl.multiple_of(n * NB, NB), NB)
            d = product(w_ref[...], y_ref[k, at, :])
            for t in range(NT_PTS):
                if first:
                    acc[t, rows, at] = d[t * MB:(t + 1) * MB]
                else:
                    acc[t, rows, at] += d[t * MB:(t + 1) * MB]

    @pl.loop(0, STEPS)
    def _(p):
        k = jnp.maximum(p - START, 0) // PER
        part = jnp.maximum(p - START, 0) % PER
        busy = p >= START

        @pl.when(jnp.logical_and(busy, part == 0))
        def _():
            for i in range(PER):
                settle(k * PER + i)

        for group in range(NG):
            for g, (actions, _last) in enumerate(PROGRAMS):
                mine = [a for a in actions if a[1] == group]
                if mine:
                    @pl.when(which == g)
                    def _():
                        for lag in sorted({a[0] for a in mine}):
                            @pl.when(jnp.logical_and(p >= lag, p < NC + lag))
                            def _():
                                for a in mine:
                                    if a[0] == lag:
                                        act(a, p - lag)

            blocks = NM // PER // NG
            for b in range(blocks):
                m = part * (NM // PER) + group * blocks + b

                @pl.when(jnp.logical_and(busy, k == 0))
                def _():
                    block(0, m, True)

                @pl.when(jnp.logical_and(busy, k > 0))
                def _():
                    block(k, m, False)

    for i in range(PER):
        settle(NC - PER + i)
    for g, (actions, _last) in enumerate(PROGRAMS):
        @pl.when(which == g)
        def _():
            @pl.loop(0, NC)
            def _(j):
                bulk_wait(send_sem.at[j], sum(len(a[5]) for a in actions))


def last_kernel(acc, x_ref, y_ref, f_ref, out, w_ref, buf, sem):
    def copy(m, slot):
        return pltpu.make_async_copy(
            buf.at[slot], out.at[:, pl.ds(pl.multiple_of(m * MB, MB), MB), :], sem.at[slot]
        )

    @pl.loop(0, NM)
    def _(m):
        slot = m % 2
        rows = pl.ds(pl.multiple_of(m * MB, MB), MB)
        weigh(x_ref[NK - 1, rows, :], lambda t: f_ref[t, NK - 1:NK, :], w_ref)

        @pl.when(m >= 2)
        def _():
            copy(m - 2, slot).wait()

        @pl.loop(0, COLS // NB)
        def _(n):
            at = pl.ds(pl.multiple_of(n * NB, NB), NB)
            d = product(w_ref[...], y_ref[NK - 1, at, :])
            for t in range(NT_PTS):
                buf[slot, t, :, at] = acc[t, rows, at] + d[t * MB:(t + 1) * MB]

        copy(m, slot).start()

    copy(NM - 2, 0).wait()
    copy(NM - 1, 1).wait()


def on_device(pair_ints, denominators, lap_points, lap_weights):
    vmem = pl.BlockSpec(memory_space=pltpu.VMEM)
    smem = pl.BlockSpec(memory_space=pltpu.SMEM)
    held = pl.pallas_call(
        gather_kernel,
        out_shape=(
            pltpu.VMEM((NT_PTS, ROWS, COLS), F32),
            pltpu.VMEM((NK, ROWS, KK), BF16),
            pltpu.VMEM((NK, COLS, KK), BF16),
            pltpu.VMEM((NT_PTS, NK, KK), F32),
        ),
        in_specs=[smem, smem, vmem, vmem],
        out_specs=(vmem,) * 4,
        scratch_shapes=[
            pltpu.VMEM((NC, NT, OWN, KC), BF16),
            pltpu.VMEM((NT_PTS * MB, KK), BF16),
            pltpu.SemaphoreType.DMA((NC,)),
            pltpu.SemaphoreType.DMA((NC, NE)),
            pltpu.SemaphoreType.DMA((NC,)),
        ],
        compiler_params=pltpu.CompilerParams(
            collective_id=0, has_side_effects=True, vmem_limit_bytes=VMEM_LIMIT
        ),
    )(lap_points, lap_weights, pair_ints, denominators.reshape(NK, KK))
    held = [pltpu.with_memory_space_constraint(a, pltpu.VMEM) for a in held]
    return pl.pallas_call(
        last_kernel,
        out_shape=jax.ShapeDtypeStruct((NT_PTS, ROWS, COLS), F32),
        in_specs=[vmem] * 4,
        out_specs=pl.BlockSpec(memory_space=pl.ANY),
        scratch_shapes=[
            pltpu.VMEM((NT_PTS * MB, KK), BF16),
            pltpu.VMEM((2, NT_PTS, MB, COLS), F32),
            pltpu.SemaphoreType.DMA((2,)),
        ],
        compiler_params=pltpu.CompilerParams(vmem_limit_bytes=VMEM_LIMIT),
    )(*held)


def solution(mesh):
    in_specs = (P(None, ("row", "col")), P(), P(), P())
    out_specs = P(None, "row", "col")
    return jax.shard_map(
        on_device, mesh=mesh, in_specs=in_specs, out_specs=out_specs, check_vma=False
    )
```

```python
import jax
import jax.numpy as jnp
from jax import lax
from jax.experimental import pallas as pl
from jax.experimental.pallas import tpu as pltpu
from jax.sharding import PartitionSpec as P

NC, NG, SMAX, NT, NE = 8, 4, 7, 6, 27
TARGETS = ((0, 12), (0, 4), (4, 2), (0, 1), (0, 2), (3, 0), (1, 1), (3, 1), (1, 0), (4, 3))
PROGRAMS = (
    (
        (
            (0, 0, -1, 0, 0, ((0, 0, 0, 3), (1, 0, 0, 4), (2, 2, 1, 5), (3, 0, 0, 0)), 1),
            (0, 1, 0, 0, 1, (), 1),
            (0, 3, 1, 2, 0, ((1, 2, 1, 8),), 0),
            (0, 3, 2, 2, 1, ((2, 1, 1, 9), (4, 1, 1, 7)), 0),
            (1, 0, 3, 0, 4, ((5, 1, 4, 9), (4, 0, 4, 8), (0, 0, 4, 7), (3, 0, 4, 4)), 1),
            (1, 0, 4, 0, 2, ((1, 0, 2, 12), (3, 0, 2, 5)), 1),
            (1, 0, 5, 0, 12, ((6, 1, 12, 8), (1, 0, 12, 10), (3, 0, 12, 6)), 0),
            (1, 1, 6, 0, 5, (), 1),
            (1, 1, 7, 0, 3, (), 1),
            (2, 0, 9, 2, 2, ((2, 1, 5, 17), (4, 1, 5, 16)), 0),
            (2, 0, 10, 0, 14, ((6, 1, 14, 16), (3, 0, 14, 10)), 0),
            (2, 1, 11, 0, 8, ((3, 0, 8, 11),), 0),
            (2, 1, 12, 2, 3, ((2, 1, 4, 20), (4, 1, 4, 17)), 0),
            (2, 1, 13, 0, 6, ((3, 0, 6, 12),), 1),
            (2, 2, 16, 0, 7, (), 1),
            (3, 0, 17, 2, 4, ((4, 1, 0, 22),), 0),
            (3, 2, 18, 0, 10, ((7, 1, 10, 22), (3, 0, 10, 16)), 0),
            (4, 2, 20, 2, 5, ((2, 1, 3, 23),), 0),
        ),
        ((8, 0, 13), (14, 0, 9), (15, 0, 15), (19, 0, 11)),
    ),
    (
        (
            (0, 0, -1, 0, 1, ((0, 0, 1, 2), (1, 0, 1, 3), (6, 1, 1, 1), (3, 0, 1, 0)), 0),
            (0, 3, 1, 0, 5, ((6, 1, 5, 6), (7, 1, 5, 7), (3, 0, 5, 6)), 0),
            (1, 0, 2, 0, 3, ((1, 0, 3, 8), (0, 0, 3, 6), (7, 1, 3, 8), (3, 0, 3, 7)), 0),
            (1, 0, 3, 0, 13, ((4, 0, 13, 5), (3, 0, 13, 8)), 1),
            (1, 2, 6, 0, 12, (), 1),
            (2, 0, 7, 0, 9, ((8, 1, 9, 14), (3, 0, 9, 14)), 1),
            (2, 1, 8, 0, 7, ((3, 0, 7, 16),), 0),
            (2, 1, 9, 0, 15, ((5, 1, 15, 16), (0, 0, 15, 15), (3, 0, 15, 15)), 1),
            (2, 2, 10, 0, 14, (), 1),
            (2, 3, 11, 0, 8, (), 1),
            (3, 1, 13, 2, 0, ((0, 2, 2, 20),), 0),
            (3, 1, 14, 2, 1, ((2, 1, 14, 17),), 0),
            (3, 2, 15, 0, 11, ((5, 1, 11, 20), (8, 1, 11, 22), (3, 0, 11, 19)), 1),
            (4, 0, 16, 0, 10, (), 1),
        ),
        ((0, 0, 0), (4, 0, 4), (5, 0, 2), (12, 0, 6)),
    ),
    (
        (
            (0, 0, -1, 0, 2, ((2, 1, 2, 1), (4, 0, 2, 4), (0, 0, 2, 2), (1, 0, 2, 2), (3, 0, 2, 0)), 0),
            (1, 0, 2, 0, 6, ((8, 2, 3, 12), (3, 0, 6, 3)), 0),
            (1, 0, 3, 0, 14, ((9, 1, 14, 10), (1, 0, 14, 10), (3, 0, 14, 4)), 0),
            (1, 3, 6, 1, 7, ((5, 1, 7, 16),), 0),
            (2, 0, 7, 1, 1, ((5, 1, 1, 18),), 0),
            (2, 1, 8, 0, 4, ((0, 0, 4, 13), (2, 1, 4, 16), (3, 0, 4, 10)), 0),
            (2, 1, 9, 2, 0, ((1, 1, 7, 17),), 0),
            (2, 1, 10, 0, 12, ((6, 2, 1, 14), (3, 0, 12, 11)), 0),
            (2, 2, 11, 0, 10, ((4, 0, 10, 18), (3, 0, 10, 12)), 0),
            (3, 3, 18, 0, 0, ((3, 0, 0, 18),), 0),
            (3, 3, 19, 0, 8, ((9, 1, 8, 23), (3, 0, 8, 19)), 0),
        ),
        ((0, 0, 3), (1, 1, 3), (4, 0, 7), (5, 0, 15), (12, 0, 13), (13, 0, 5), (14, 0, 11), (15, 1, 2), (16, 1, 5), (17, 1, 4), (20, 0, 9), (21, 0, 1), (22, 1, 0), (23, 1, 6)),
    ),
    (
        (
            (0, 0, -1, 0, 3, ((0, 0, 3, 2), (1, 0, 3, 2), (6, 2, 1, 2), (4, 0, 3, 2), (3, 0, 3, 0)), 0),
            (1, 0, 1, 0, 7, ((6, 2, 2, 9), (4, 0, 7, 8), (3, 0, 7, 4)), 0),
            (1, 0, 2, 0, 15, ((4, 0, 15, 9), (1, 0, 15, 8), (3, 0, 15, 5)), 0),
            (2, 1, 5, 0, 13, ((3, 0, 13, 12),), 0),
            (2, 1, 6, 0, 5, ((9, 1, 5, 17), (0, 0, 5, 14), (3, 0, 5, 13)), 0),
            (2, 1, 7, 0, 11, ((2, 1, 11, 19), (3, 0, 11, 14)), 0),
            (2, 1, 8, 1, 14, ((5, 1, 14, 16),), 0),
            (2, 1, 9, 2, 0, ((1, 1, 14, 17),), 0),
            (3, 0, 13, 2, 1, ((0, 1, 12, 16),), 0),
            (3, 1, 14, 1, 11, ((5, 1, 11, 18),), 0),
            (3, 1, 15, 0, 9, ((3, 0, 9, 20),), 0),
            (3, 1, 16, 1, 12, ((5, 1, 12, 20),), 0),
            (3, 2, 17, 0, 1, ((7, 2, 3, 21), (6, 2, 5, 20), (3, 0, 1, 21)), 0),
            (4, 2, 21, 2, 2, ((0, 1, 15, 22),), 0),
        ),
        ((0, 0, 2), (3, 0, 6), (4, 0, 14), (10, 0, 4), (11, 0, 12), (12, 0, 10), (18, 0, 0), (19, 0, 8), (20, 1, 15), (22, 1, 9), (23, 1, 13), (24, 1, 10), (25, 1, 8)),
    ),
    (
        (
            (0, 0, -1, 0, 4, ((1, 0, 4, 3), (0, 0, 4, 3), (4, 0, 4, 1), (3, 0, 4, 0)), 0),
            (1, 0, 1, 2, 0, ((0, 1, 6, 9),), 0),
            (1, 1, 2, 0, 8, ((4, 0, 8, 13), (7, 2, 0, 9), (1, 0, 8, 11), (3, 0, 8, 4)), 0),
            (1, 1, 3, 0, 6, ((1, 0, 6, 13), (3, 0, 6, 6)), 0),
            (1, 1, 4, 0, 0, ((4, 0, 0, 12), (0, 0, 0, 13), (3, 0, 0, 5)), 0),
            (1, 3, 8, 2, 1, ((2, 1, 1, 12),), 0),
            (1, 3, 9, 2, 2, ((0, 1, 4, 16),), 0),
            (2, 2, 10, 0, 12, ((3, 0, 12, 10),), 0),
            (2, 2, 12, 0, 2, ((0, 0, 2, 20), (3, 0, 2, 11)), 0),
            (2, 2, 14, 0, 10, ((3, 0, 10, 12),), 0),
            (3, 1, 17, 0, 14, ((3, 0, 14, 17),), 0),
            (3, 1, 19, 1, 0, ((2, 2, 1, 19),), 0),
            (4, 2, 21, 2, 3, ((2, 1, 7, 25), (8, 2, 1, 22)), 0),
            (5, 2, 22, 1, 6, ((8, 1, 6, 24),), 0),
        ),
        ((0, 0, 5), (5, 0, 9), (6, 0, 1), (7, 0, 7), (11, 0, 13), (13, 0, 3), (15, 0, 11), (16, 1, 1), (18, 1, 7), (20, 0, 15), (23, 1, 3), (24, 1, 2), (25, 1, 4), (26, 1, 5)),
    ),
    (
        (
            (0, 0, -1, 0, 5, ((4, 0, 5, 1), (1, 0, 5, 1), (0, 0, 5, 4), (3, 0, 5, 0)), 0),
            (1, 0, 1, 0, 9, ((4, 0, 9, 10), (3, 0, 9, 5)), 0),
            (1, 0, 2, 0, 7, ((3, 0, 7, 7),), 0),
            (1, 0, 3, 0, 1, ((7, 2, 0, 9), (4, 0, 1, 11), (3, 0, 1, 6)), 0),
            (2, 0, 7, 0, 13, ((3, 0, 13, 11),), 0),
            (2, 1, 8, 0, 3, ((3, 0, 3, 13),), 0),
            (2, 2, 9, 0, 11, ((3, 0, 11, 15),), 0),
            (3, 1, 13, 1, 9, ((5, 1, 9, 20),), 0),
            (3, 1, 14, 2, 0, ((8, 2, 1, 19), (2, 1, 11, 17)), 0),
            (3, 1, 15, 0, 15, ((3, 0, 15, 20),), 0),
            (3, 2, 16, 1, 8, ((2, 2, 0, 18), (8, 1, 8, 21)), 0),
            (4, 2, 18, 1, 13, ((8, 1, 13, 23),), 0),
            (4, 2, 19, 1, 11, ((5, 1, 11, 23),), 0),
            (4, 2, 20, 1, 10, ((8, 1, 10, 24),), 0),
            (4, 3, 21, 1, 12, ((5, 1, 12, 24),), 0),
            (6, 0, 23, 1, 14, ((5, 1, 14, 25),), 0),
        ),
        ((0, 0, 4), (4, 0, 8), (5, 0, 0), (6, 0, 6), (10, 0, 12), (11, 0, 2), (12, 0, 10), (17, 0, 14), (22, 1, 15)),
    ),
    (
        (
            (0, 0, -1, 0, 6, ((1, 0, 6, 2), (0, 0, 6, 3), (4, 0, 6, 3), (3, 0, 6, 0)), 0),
            (1, 0, 1, 0, 4, ((3, 0, 4, 4),), 0),
            (1, 0, 2, 0, 2, ((3, 0, 2, 5),), 0),
            (1, 1, 3, 0, 10, ((9, 2, 0, 8), (3, 0, 10, 6)), 0),
            (2, 1, 9, 1, 2, ((8, 1, 2, 19), (2, 2, 0, 13)), 0),
            (2, 2, 10, 0, 14, ((3, 0, 14, 12),), 0),
            (2, 2, 12, 0, 0, ((0, 0, 0, 15), (1, 0, 0, 18), (3, 0, 0, 13)), 0),
            (2, 2, 13, 0, 8, ((1, 0, 8, 19), (3, 0, 8, 14)), 0),
            (3, 2, 16, 0, 12, ((3, 0, 12, 18),), 0),
            (5, 3, 20, 2, 0, ((4, 1, 2, 24),), 0),
            (5, 3, 22, 2, 1, ((2, 1, 5, 25), (4, 1, 5, 26)), 0),
        ),
        ((0, 0, 7), (4, 0, 5), (5, 0, 3), (6, 0, 11), (7, 1, 3), (8, 1, 5), (11, 0, 15), (14, 0, 9), (15, 0, 1), (17, 1, 7), (18, 0, 13), (19, 1, 1), (21, 1, 6), (23, 1, 0), (24, 1, 4)),
    ),
    (
        (
            (0, 0, -1, 0, 7, ((7, 2, 0, 1), (1, 0, 7, 1), (0, 0, 7, 4), (4, 0, 7, 2), (3, 0, 7, 0)), 0),
            (1, 0, 1, 0, 5, ((1, 0, 5, 6), (0, 0, 5, 12), (3, 0, 5, 4)), 0),
            (1, 0, 2, 0, 3, ((0, 0, 3, 13), (3, 0, 3, 5)), 0),
            (1, 0, 3, 0, 11, ((1, 0, 11, 7), (3, 0, 11, 6)), 0),
            (2, 0, 7, 1, 11, ((4, 2, 0, 14), (8, 1, 11, 13)), 0),
            (2, 1, 8, 0, 15, ((4, 0, 15, 15), (3, 0, 15, 11)), 0),
            (2, 1, 9, 2, 0, ((5, 2, 0, 13),), 0),
            (2, 1, 10, 0, 9, ((2, 2, 1, 13), (3, 0, 9, 14)), 0),
            (2, 1, 11, 0, 1, ((3, 0, 1, 15),), 0),
            (3, 1, 15, 0, 13, ((3, 0, 13, 18),), 0),
            (3, 1, 16, 1, 9, ((8, 1, 9, 19),), 0),
            (3, 3, 17, 1, 14, ((8, 1, 14, 21),), 0),
            (4, 2, 19, 2, 1, ((2, 1, 9, 19),), 0),
            (4, 2, 20, 1, 13, ((8, 1, 13, 22),), 0),
            (4, 3, 22, 1, 12, ((8, 1, 12, 23),), 0),
        ),
        ((0, 0, 6), (4, 0, 4), (5, 0, 2), (6, 0, 10), (12, 0, 14), (13, 0, 0), (14, 0, 8), (18, 0, 12), (21, 1, 10), (23, 1, 15), (24, 1, 8)),
    ),
    (
        (
            (0, 0, -1, 0, 8, ((0, 0, 8, 2), (4, 0, 8, 2), (1, 0, 8, 2), (3, 0, 8, 0)), 0),
            (1, 0, 1, 0, 12, ((3, 0, 12, 5),), 0),
            (1, 1, 2, 0, 10, ((1, 0, 10, 9), (0, 0, 10, 14), (3, 0, 10, 7)), 0),
            (1, 1, 3, 0, 4, ((4, 0, 4, 9), (3, 0, 4, 6)), 0),
            (2, 0, 7, 2, 0, ((2, 2, 1, 13),), 0),
            (2, 0, 8, 0, 14, ((0, 0, 14, 17), (3, 0, 14, 12)), 0),
            (2, 1, 9, 1, 6, ((8, 1, 6, 13), (5, 1, 6, 15)), 0),
            (2, 1, 10, 1, 7, ((5, 1, 7, 14), (8, 1, 7, 14)), 0),
            (2, 2, 12, 0, 6, ((1, 0, 6, 14), (3, 0, 6, 13)), 0),
            (2, 2, 13, 0, 0, ((3, 0, 0, 14),), 0),
            (3, 2, 17, 2, 1, ((2, 2, 2, 21),), 0),
            (3, 2, 18, 1, 3, ((5, 1, 3, 19),), 0),
            (3, 2, 19, 1, 2, ((5, 1, 2, 20),), 0),
            (3, 3, 20, 0, 2, ((3, 0, 2, 19),), 0),
            (4, 2, 22, 1, 0, ((8, 1, 0, 19), (5, 1, 0, 21)), 0),
            (4, 3, 23, 1, 1, ((8, 1, 1, 20), (5, 1, 1, 22)), 0),
        ),
        ((0, 0, 9), (4, 0, 13), (5, 0, 5), (6, 0, 11), (11, 0, 15), (14, 0, 7), (15, 0, 1), (16, 1, 4), (21, 0, 3), (24, 1, 5)),
    ),
    (
        (
            (0, 0, -1, 0, 9, ((0, 0, 9, 1), (1, 0, 9, 1), (4, 0, 9, 3), (3, 0, 9, 0)), 0),
            (1, 0, 1, 1, 11, ((8, 1, 11, 11),), 0),
            (1, 0, 2, 0, 13, ((4, 0, 13, 10), (0, 0, 13, 7), (3, 0, 13, 4)), 0),
            (1, 0, 3, 0, 11, ((1, 0, 11, 7), (0, 0, 11, 9), (3, 0, 11, 6)), 0),
            (1, 0, 4, 0, 5, ((1, 0, 5, 8), (3, 0, 5, 5)), 0),
            (2, 0, 8, 0, 15, ((3, 0, 15, 11),), 0),
            (2, 0, 9, 2, 0, ((2, 1, 11, 15), (4, 1, 11, 18)), 0),
            (2, 1, 10, 0, 7, ((3, 0, 7, 14),), 0),
            (2, 1, 11, 0, 1, ((3, 0, 1, 15),), 0),
            (3, 2, 17, 1, 12, ((8, 1, 12, 22),), 0),
            (3, 2, 18, 0, 3, ((3, 0, 3, 21),), 0),
            (5, 2, 22, 2, 1, ((2, 1, 15, 23),), 0),
        ),
        ((0, 0, 8), (5, 0, 12), (6, 0, 4), (7, 0, 10), (12, 0, 14), (13, 0, 6), (14, 0, 0), (15, 1, 10), (16, 1, 13), (19, 0, 2), (20, 1, 14), (21, 1, 15), (23, 1, 9), (24, 1, 8)),
    ),
    (
        (
            (0, 0, -1, 0, 10, ((0, 0, 10, 3), (1, 0, 10, 3), (4, 0, 10, 2), (3, 0, 10, 0)), 0),
            (1, 0, 1, 0, 14, ((3, 0, 14, 6),), 0),
            (1, 0, 2, 0, 8, ((1, 0, 8, 8), (3, 0, 8, 7)), 0),
            (1, 0, 3, 0, 6, ((4, 0, 6, 12), (1, 0, 6, 9), (3, 0, 6, 8)), 0),
            (2, 1, 7, 0, 12, ((0, 0, 12, 16), (3, 0, 12, 14)), 0),
            (2, 1, 8, 0, 2, ((3, 0, 2, 15),), 0),
            (2, 2, 9, 0, 4, ((3, 0, 4, 16),), 0),
            (3, 2, 13, 1, 4, ((5, 1, 4, 17),), 0),
            (3, 3, 15, 0, 0, ((3, 0, 0, 21),), 0),
            (4, 2, 17, 1, 7, ((8, 1, 7, 24),), 0),
            (4, 3, 18, 2, 0, ((0, 1, 0, 23),), 0),
            (5, 3, 19, 1, 2, ((5, 1, 2, 23),), 0),
            (6, 0, 20, 1, 3, ((5, 1, 3, 24),), 0),
        ),
        ((0, 0, 11), (4, 0, 15), (5, 0, 9), (6, 0, 7), (10, 0, 13), (11, 0, 5), (12, 0, 3), (14, 1, 5), (16, 0, 1), (21, 1, 6), (22, 1, 0), (23, 1, 1)),
    ),
    (
        (
            (0, 0, -1, 0, 11, ((0, 0, 11, 3), (4, 0, 11, 3), (1, 0, 11, 3), (3, 0, 11, 0)), 0),
            (0, 3, 1, 0, 15, ((4, 0, 15, 8), (3, 0, 15, 4)), 0),
            (1, 0, 2, 2, 0, ((0, 1, 11, 7),), 0),
            (1, 0, 3, 0, 9, ((1, 0, 9, 7), (3, 0, 9, 5)), 0),
            (1, 0, 4, 0, 7, ((1, 0, 7, 9), (4, 0, 7, 10), (3, 0, 7, 6)), 0),
            (1, 0, 5, 2, 1, ((8, 2, 0, 9),), 0),
            (2, 0, 9, 1, 8, ((8, 1, 8, 15),), 0),
            (2, 0, 10, 0, 13, ((0, 0, 13, 15), (3, 0, 13, 10)), 0),
            (2, 0, 11, 1, 9, ((5, 1, 9, 12), (2, 2, 4, 17)), 0),
            (2, 0, 12, 0, 5, ((3, 0, 5, 11),), 0),
            (2, 1, 13, 0, 3, ((4, 0, 3, 18), (3, 0, 3, 12)), 0),
            (3, 1, 17, 1, 12, ((8, 1, 12, 20),), 0),
            (3, 1, 19, 0, 1, ((3, 0, 1, 16),), 0),
            (3, 2, 20, 1, 13, ((5, 1, 13, 19), (8, 1, 13, 21)), 0),
            (4, 2, 22, 1, 14, ((5, 1, 14, 22),), 0),
        ),
        ((0, 0, 10), (6, 0, 14), (7, 0, 8), (8, 0, 6), (14, 0, 12), (15, 0, 2), (16, 0, 4), (18, 1, 11), (21, 0, 0), (23, 1, 10), (24, 1, 15)),
    ),
    (
        (
            (0, 0, -1, 0, 12, ((0, 0, 12, 5), (4, 0, 12, 1), (1, 0, 12, 1), (3, 0, 12, 0)), 0),
            (0, 3, 1, 0, 14, ((0, 0, 14, 10), (1, 0, 14, 8), (3, 0, 14, 3)), 0),
            (1, 0, 2, 0, 8, ((3, 0, 8, 4),), 0),
            (1, 1, 3, 0, 0, ((4, 0, 0, 7), (2, 2, 0, 9), (3, 0, 0, 5)), 0),
            (2, 1, 6, 0, 2, ((3, 0, 2, 9),), 0),
            (2, 1, 7, 0, 4, ((3, 0, 4, 10),), 0),
            (2, 1, 8, 2, 0, ((1, 1, 3, 18),), 0),
            (2, 2, 9, 0, 10, ((3, 0, 10, 11),), 0),
            (3, 1, 13, 2, 1, ((1, 1, 0, 22),), 0),
            (3, 2, 14, 0, 6, ((5, 2, 0, 18), (3, 0, 6, 16)), 0),
            (5, 2, 19, 1, 0, ((5, 1, 0, 21),), 0),
            (5, 3, 20, 1, 1, ((8, 1, 1, 23),), 0),
            (5, 3, 21, 1, 7, ((5, 1, 7, 23),), 0),
            (6, 0, 22, 1, 6, ((5, 1, 6, 22),), 0),
        ),
        ((0, 0, 13), (4, 0, 9), (5, 0, 1), (10, 0, 3), (11, 0, 11), (12, 0, 5), (15, 0, 7), (16, 0, 15), (17, 1, 2), (18, 1, 3), (23, 1, 4), (24, 1, 5)),
    ),
    (
        (
            (0, 0, -1, 0, 13, ((5, 2, 0, 2), (1, 0, 13, 2), (4, 0, 13, 1), (0, 0, 13, 3), (3, 0, 13, 0)), 0),
            (0, 3, 1, 0, 9, ((0, 0, 9, 7), (3, 0, 9, 4)), 0),
            (1, 0, 2, 0, 1, ((4, 0, 1, 8), (1, 0, 1, 11), (3, 0, 1, 5)), 0),
            (2, 1, 6, 0, 3, ((3, 0, 3, 10),), 0),
            (2, 1, 7, 0, 11, ((0, 0, 11, 15), (3, 0, 11, 11)), 0),
            (2, 1, 8, 0, 5, ((3, 0, 5, 12),), 0),
            (3, 0, 12, 1, 15, ((4, 2, 0, 18), (8, 1, 15, 17)), 0),
            (3, 1, 13, 2, 0, ((4, 1, 11, 20),), 0),
            (3, 1, 14, 0, 7, ((3, 0, 7, 15),), 0),
            (3, 1, 15, 0, 15, ((3, 0, 15, 16),), 0),
            (4, 1, 18, 2, 1, ((8, 2, 2, 21), (2, 1, 8, 19)), 0),
            (4, 2, 19, 1, 11, ((2, 2, 0, 20), (8, 1, 11, 23)), 0),
            (4, 2, 20, 2, 2, ((8, 2, 3, 24), (2, 1, 15, 21)), 0),
            (5, 3, 22, 1, 8, ((8, 1, 8, 26),), 0),
            (5, 3, 23, 1, 9, ((5, 1, 9, 24),), 0),
        ),
        ((0, 0, 12), (3, 0, 14), (4, 0, 8), (5, 0, 0), (9, 0, 2), (10, 0, 4), (11, 0, 10), (16, 0, 6), (17, 1, 10), (21, 1, 14), (24, 1, 13), (25, 1, 12)),
    ),
    (
        (
            (0, 0, -1, 0, 14, ((4, 0, 14, 1), (0, 0, 14, 3), (1, 0, 14, 1), (3, 0, 14, 0)), 0),
            (1, 0, 1, 0, 12, ((0, 0, 12, 10), (1, 0, 12, 7), (3, 0, 12, 4)), 0),
            (1, 0, 2, 0, 2, ((1, 0, 2, 8), (4, 0, 2, 6), (3, 0, 2, 5)), 0),
            (1, 0, 3, 0, 10, ((0, 0, 10, 11), (3, 0, 10, 6)), 0),
            (2, 1, 7, 0, 0, ((5, 2, 1, 17), (3, 0, 0, 10)), 0),
            (2, 2, 8, 0, 8, ((3, 0, 8, 11),), 0),
            (2, 2, 9, 0, 6, ((3, 0, 6, 13),), 0),
            (3, 1, 13, 0, 4, ((3, 0, 4, 15),), 0),
            (3, 2, 14, 1, 1, ((8, 1, 1, 18),), 0),
            (4, 2, 18, 2, 0, ((4, 1, 1, 20),), 0),
            (4, 3, 19, 1, 5, ((8, 1, 5, 21),), 0),
            (4, 3, 20, 1, 4, ((8, 1, 4, 22),), 0),
        ),
        ((0, 0, 15), (4, 0, 13), (5, 0, 3), (6, 0, 11), (10, 0, 9), (11, 0, 1), (12, 0, 7), (15, 1, 0), (16, 0, 5), (17, 1, 2), (21, 1, 6), (22, 1, 7), (23, 1, 3)),
    ),
    (
        (
            (0, 0, -1, 0, 15, ((0, 0, 15, 2), (2, 2, 0, 1), (1, 0, 15, 1), (3, 0, 15, 0)), 0),
            (0, 3, 1, 0, 13, ((2, 2, 2, 9), (3, 0, 13, 4)), 0),
            (0, 3, 2, 0, 3, ((7, 2, 0, 7), (3, 0, 3, 5)), 0),
            (1, 0, 3, 0, 11, ((3, 0, 11, 6),), 0),
            (2, 0, 7, 0, 9, ((0, 0, 9, 15), (3, 0, 9, 10)), 0),
            (2, 0, 8, 0, 1, ((0, 0, 1, 17), (1, 0, 1, 19), (3, 0, 1, 11)), 0),
            (2, 1, 9, 0, 7, ((4, 0, 7, 14), (3, 0, 7, 12)), 0),
            (3, 0, 12, 1, 8, ((4, 2, 1, 18), (8, 1, 8, 17)), 0),
            (3, 1, 14, 0, 5, ((3, 0, 5, 16),), 0),
            (4, 1, 16, 1, 12, ((8, 1, 12, 21),), 0),
            (4, 1, 18, 2, 0, ((2, 1, 15, 22),), 0),
            (4, 2, 19, 2, 1, ((5, 2, 1, 22), (4, 1, 9, 23)), 0),
            (5, 1, 21, 2, 2, ((2, 1, 10, 23),), 0),
            (5, 3, 22, 1, 15, ((5, 1, 15, 23), (8, 1, 15, 24)), 0),
            (5, 3, 24, 2, 3, ((2, 1, 13, 25),), 0),
            (5, 3, 25, 1, 14, ((5, 1, 14, 24),), 0),
        ),
        ((0, 0, 14), (4, 0, 12), (5, 0, 2), (6, 0, 10), (10, 0, 0), (11, 0, 8), (13, 0, 6), (15, 0, 4), (17, 1, 13), (20, 1, 11), (23, 1, 9), (26, 1, 10)),
    ),
)
VMEM_LIMIT = 24 << 20
MBV, NBV = 256, 1024

F32, BF16 = jnp.float32, jnp.bfloat16
MESH = pl.DeviceIdType.MESH
NT_PTS = 3
PAIRS, ROWS, COLS, OWN = 2048, 2048, 1024, 128
KC = PAIRS // NC
KK = 512
NK = PAIRS // KK
PER = KK // KC
MB, NB = MBV, NBV
NM = ROWS // MB
START = SMAX + PER
STEPS = NC + SMAX


def flip(value, bits):
    return [jnp.int32(b) * (1 - 2 * ((value // b) % 2)) for b in bits]


def flipped(value, deltas, bits, mask):
    for delta, bit in zip(deltas, bits):
        if mask & bit:
            value = value + delta
    return value


def weigh(x, factor, w_ref):
    x = x.astype(F32)
    for t in range(NT_PTS):
        w_ref[pl.ds(t * MB, MB), :] = (x * factor(t)).astype(BF16)


def product(w, y):
    return lax.dot_general(w, y, (((1,), (1,)), ((), ())), preferred_element_type=F32)


def gather_kernel(points, weights, own_ref, den_ref, acc, x_ref, y_ref, f_ref,
                  transit, w_ref, send_sem, recv_sem, local_sem):
    row, col = lax.axis_index("row"), lax.axis_index("col")
    row_d, col_d = flip(row, (1, 2, 4)), flip(col, (1, 2, 4, 8))
    peers = [
        {"row": flipped(row, row_d, (1, 2, 4), dr), "col": flipped(col, col_d, (1, 2, 4, 8), dc)}
        for dr, dc in TARGETS
    ]
    barrier = pltpu.get_barrier_semaphore()
    for peer in peers:
        pl.semaphore_signal(barrier, inc=1, device_id=peer, device_id_type=MESH)

    high = row // 4
    code = row * 2 + high
    code_d = flip(code, (1, 2, 4, 8))

    def lanes(j):
        return pl.ds(pl.multiple_of((j % PER) * KC, KC), KC)

    def place(kind, mark, j):
        if kind == 2:
            return transit.at[j, mark]
        slot = flipped(code, code_d, (1, 2, 4, 8), mark)
        if kind == 0:
            return x_ref.at[j // PER, pl.ds(pl.multiple_of(slot * OWN, OWN), OWN), lanes(j)]
        slot = slot % 8
        return y_ref.at[j // PER, pl.ds(pl.multiple_of(slot * OWN, OWN), OWN), lanes(j)]

    for k in range(NK):
        x_ref[k, pl.ds(pl.multiple_of(col * OWN, OWN), OWN), :] = own_ref[pl.ds(k * KK, KK), :].T
    for t in range(NT_PTS):
        f_ref[t] = weights[t] * jnp.exp(-points[t] * den_ref[...])
    pl.semaphore_wait(barrier, len(TARGETS))

    k_col = col // 2
    bits = [((row // b) % 2 + (k_col // b) % 2) % 2 for b in (4, 2, 1)]
    which = (bits[0] * 4 + bits[1] * 2 + bits[2]) * 2 + ((col % 2) + high) % 2

    def arrived(kind, mark, event, j):
        ref = place(kind, mark, j)
        pltpu.make_async_copy(ref, ref, recv_sem.at[j, event]).wait()

    def act(action, j):
        _, _, event, kind, mark, kids, local = action
        if event >= 0:
            arrived(kind, mark, event, j)
        src = place(kind, mark, j)
        for target, to_kind, to_mark, to_event in kids:
            pltpu.make_async_remote_copy(
                src_ref=src, dst_ref=place(to_kind, to_mark, j),
                send_sem=send_sem.at[j], recv_sem=recv_sem.at[j, to_event],
                device_id=peers[target], device_id_type=MESH,
            ).start()
        if local:
            pltpu.make_async_copy(src, place(1, mark, j), local_sem.at[j]).start()

    def bulk_wait(sem, copies):
        ref = acc.at[0, pl.ds(0, copies * OWN * KC // (2 * COLS)), :]
        pltpu.make_async_copy(ref, ref, sem).wait()

    def settle(j):
        for g, (actions, last) in enumerate(PROGRAMS):
            @pl.when(which == g)
            def _():
                for event, kind, mark in last:
                    arrived(kind, mark, event, j)
                copies = sum(a[6] for a in actions)
                if copies:
                    bulk_wait(local_sem.at[j], copies)

    def block(k, m):
        rows = pl.ds(pl.multiple_of(m * MB, MB), MB)
        weigh(x_ref[k, rows, :], lambda t: f_ref[t, pl.ds(k, 1), :], w_ref)

        @pl.loop(0, COLS // NB)
        def _(n):
            at = pl.ds(pl.multiple_of(n * NB, NB), NB)
            for t in range(NT_PTS):
                acc[t, rows, at] += product(w_ref[pl.ds(t * MB, MB), :], y_ref[k, at, :])

    @pl.loop(0, STEPS)
    def _(p):
        k = jnp.maximum(p - START, 0) // PER
        part = jnp.maximum(p - START, 0) % PER
        busy = p >= START

        @pl.when(jnp.logical_and(busy, part == 0))
        def _():
            for i in range(PER):
                settle(k * PER + i)

        @pl.loop(0, NG)
        def _(group):
            for g, (actions, _last) in enumerate(PROGRAMS):
                @pl.when(which == g)
                def _():
                    for at in range(NG):
                        mine = [a for a in actions if a[1] == at]
                        for lag in sorted({a[0] for a in mine}):
                            @pl.when(jnp.logical_and(group == at, jnp.logical_and(p >= lag, p < NC + lag)))
                            def _():
                                for a in mine:
                                    if a[0] == lag:
                                        act(a, p - lag)

            @pl.when(jnp.logical_and(p == 0, group == 0))
            def _():
                @pl.loop(0, ROWS // 64)
                def _(m):
                    at = pl.ds(pl.multiple_of(m * 64, 64), 64)
                    acc[:, at, :] = jnp.zeros((NT_PTS, 64, COLS), F32)

            @pl.when(busy)
            def _():
                for b in range(NM // PER // NG):
                    block(k, (part * NG + group) * (NM // PER // NG) + b)

    for i in range(PER):
        settle(NC - PER + i)
    for g, (actions, _last) in enumerate(PROGRAMS):
        @pl.when(which == g)
        def _():
            @pl.loop(0, NC)
            def _(j):
                bulk_wait(send_sem.at[j], sum(len(a[5]) for a in actions))


def last_kernel(acc, x_ref, y_ref, f_ref, out, w_ref, buf, sem):
    def copy(m, slot):
        return pltpu.make_async_copy(
            buf.at[slot], out.at[:, pl.ds(pl.multiple_of(m * MB, MB), MB), :], sem.at[slot]
        )

    @pl.loop(0, NM)
    def _(m):
        slot = m % 2
        rows = pl.ds(pl.multiple_of(m * MB, MB), MB)
        weigh(x_ref[NK - 1, rows, :], lambda t: f_ref[t, NK - 1:NK, :], w_ref)

        @pl.when(m >= 2)
        def _():
            copy(m - 2, slot).wait()

        @pl.loop(0, COLS // NB)
        def _(n):
            at = pl.ds(pl.multiple_of(n * NB, NB), NB)
            for t in range(NT_PTS):
                d = product(w_ref[pl.ds(t * MB, MB), :], y_ref[NK - 1, at, :])
                buf[slot, t, :, at] = acc[t, rows, at] + d

        copy(m, slot).start()

    copy(NM - 2, 0).wait()
    copy(NM - 1, 1).wait()


def on_device(pair_ints, denominators, lap_points, lap_weights):
    vmem = pl.BlockSpec(memory_space=pltpu.VMEM)
    smem = pl.BlockSpec(memory_space=pltpu.SMEM)
    held = pl.pallas_call(
        gather_kernel,
        out_shape=(
            pltpu.VMEM((NT_PTS, ROWS, COLS), F32),
            pltpu.VMEM((NK, ROWS, KK), BF16),
            pltpu.VMEM((NK, COLS, KK), BF16),
            pltpu.VMEM((NT_PTS, NK, KK), F32),
        ),
        in_specs=[smem, smem, vmem, vmem],
        out_specs=(vmem,) * 4,
        scratch_shapes=[
            pltpu.VMEM((NC, NT, OWN, KC), BF16),
            pltpu.VMEM((NT_PTS * MB, KK), BF16),
            pltpu.SemaphoreType.DMA((NC,)),
            pltpu.SemaphoreType.DMA((NC, NE)),
            pltpu.SemaphoreType.DMA((NC,)),
        ],
        compiler_params=pltpu.CompilerParams(
            collective_id=0, has_side_effects=True, vmem_limit_bytes=VMEM_LIMIT
        ),
    )(lap_points, lap_weights, pair_ints, denominators.reshape(NK, KK))
    held = [pltpu.with_memory_space_constraint(a, pltpu.VMEM) for a in held]
    return pl.pallas_call(
        last_kernel,
        out_shape=jax.ShapeDtypeStruct((NT_PTS, ROWS, COLS), F32),
        in_specs=[vmem] * 4,
        out_specs=pl.BlockSpec(memory_space=pl.ANY),
        scratch_shapes=[
            pltpu.VMEM((NT_PTS * MB, KK), BF16),
            pltpu.VMEM((2, NT_PTS, MB, COLS), F32),
            pltpu.SemaphoreType.DMA((2,)),
        ],
        compiler_params=pltpu.CompilerParams(vmem_limit_bytes=VMEM_LIMIT),
    )(*held)


def solution(mesh):
    in_specs = (P(None, ("row", "col")), P(), P(), P())
    out_specs = P(None, "row", "col")
    return jax.shard_map(
        on_device, mesh=mesh, in_specs=in_specs, out_specs=out_specs, check_vma=False
    )
```

```python
import itertools

import jax
import jax.numpy as jnp
from jax import lax
from jax.experimental import pallas as pl
from jax.experimental.pallas import tpu as pltpu
from jax.sharding import PartitionSpec as P

NC, NG, SMAX, NT, NE = 8, 2, 8, 6, 27
TARGETS = ((0, 12), (0, 4), (4, 2), (0, 1), (3, 0), (0, 2), (1, 1), (3, 1), (1, 0), (4, 3))
PROGRAMS = (
    (
        (
            (0, 0, -1, 0, 0, ((0, 0, 0, 2), (1, 0, 0, 5), (2, 2, 1, 5), (3, 0, 0, 0)), 1),
            (1, 0, 1, 2, 0, ((1, 2, 1, 8),), 0),
            (4, 0, 18, 0, 10, ((7, 1, 10, 22), (3, 0, 10, 16)), 0),
            (3, 0, 15, 0, 7, (), 1),
            (1, 0, 2, 0, 4, ((4, 1, 4, 8), (5, 0, 4, 7), (0, 0, 4, 6), (3, 0, 4, 4)), 1),
            (1, 0, 3, 2, 1, ((2, 1, 1, 10), (5, 1, 1, 9)), 0),
            (2, 0, 9, 0, 14, ((6, 1, 14, 15), (3, 0, 14, 10)), 0),
            (1, 0, 4, 0, 2, ((1, 0, 2, 11), (3, 0, 2, 6)), 1),
            (2, 0, 10, 2, 2, ((2, 1, 5, 18), (5, 1, 5, 16)), 0),
            (1, 0, 5, 0, 12, ((6, 1, 12, 6), (1, 0, 12, 10), (3, 0, 12, 5)), 0),
            (0, 0, 0, 0, 1, (), 1),
            (2, 0, 11, 0, 6, ((3, 0, 6, 11),), 1),
            (1, 0, 6, 0, 5, (), 1),
            (2, 1, 12, 0, 8, ((3, 0, 8, 12),), 0),
            (3, 1, 17, 2, 4, ((5, 1, 0, 22),), 0),
            (2, 1, 13, 2, 3, ((2, 1, 4, 20), (5, 1, 4, 17)), 0),
            (1, 1, 8, 0, 3, (), 1),
            (4, 1, 20, 2, 5, ((2, 1, 3, 23),), 0),
        ),
        ((7, 0, 13), (14, 0, 15), (16, 0, 9), (19, 0, 11)),
    ),
    (
        (
            (0, 0, -1, 0, 1, ((0, 0, 1, 1), (1, 0, 1, 3), (6, 1, 1, 2), (3, 0, 1, 0)), 0),
            (1, 0, 1, 0, 5, ((6, 1, 5, 6), (7, 1, 5, 7), (3, 0, 5, 6)), 0),
            (3, 0, 12, 0, 8, (), 1),
            (1, 0, 2, 0, 3, ((1, 0, 3, 8), (0, 0, 3, 7), (7, 1, 3, 9), (3, 0, 3, 8)), 0),
            (1, 0, 3, 0, 13, ((5, 0, 13, 5), (3, 0, 13, 7)), 1),
            (2, 0, 7, 0, 15, ((4, 1, 15, 15), (0, 0, 15, 13), (3, 0, 15, 14)), 1),
            (4, 1, 16, 0, 10, (), 1),
            (2, 1, 8, 0, 7, ((3, 0, 7, 15),), 0),
            (2, 1, 9, 0, 9, ((8, 1, 9, 16), (3, 0, 9, 16)), 1),
            (3, 1, 13, 2, 0, ((0, 2, 2, 19),), 0),
            (3, 1, 14, 2, 1, ((2, 1, 14, 17),), 0),
            (2, 1, 10, 0, 14, (), 1),
            (1, 1, 5, 0, 12, (), 1),
            (3, 1, 15, 0, 11, ((4, 1, 11, 20), (8, 1, 11, 22), (3, 0, 11, 19)), 1),
        ),
        ((0, 0, 0), (4, 0, 4), (6, 0, 2), (11, 0, 6)),
    ),
    (
        (
            (0, 0, -1, 0, 2, ((2, 1, 2, 1), (5, 0, 2, 4), (0, 0, 2, 1), (1, 0, 2, 1), (3, 0, 2, 0)), 0),
            (2, 0, 6, 1, 7, ((4, 1, 7, 16),), 0),
            (1, 0, 1, 0, 14, ((9, 1, 14, 10), (1, 0, 14, 10), (3, 0, 14, 3)), 0),
            (1, 0, 3, 0, 6, ((8, 2, 3, 13), (3, 0, 6, 4)), 0),
            (4, 0, 20, 0, 8, ((9, 1, 8, 23), (3, 0, 8, 18)), 0),
            (4, 0, 21, 0, 0, ((3, 0, 0, 19),), 0),
            (2, 0, 7, 0, 4, ((0, 0, 4, 13), (2, 1, 4, 16), (3, 0, 4, 10)), 0),
            (2, 1, 8, 0, 12, ((6, 2, 1, 14), (3, 0, 12, 11)), 0),
            (2, 1, 9, 1, 1, ((4, 1, 1, 19),), 0),
            (2, 1, 10, 2, 0, ((1, 1, 7, 17),), 0),
            (2, 1, 11, 0, 10, ((5, 0, 10, 18), (3, 0, 10, 12)), 0),
        ),
        ((0, 0, 3), (2, 1, 3), (4, 0, 15), (5, 0, 7), (12, 0, 13), (13, 0, 11), (14, 0, 5), (15, 1, 2), (16, 1, 5), (17, 1, 4), (18, 0, 1), (19, 0, 9), (22, 1, 0), (23, 1, 6)),
    ),
    (
        (
            (0, 0, -1, 0, 3, ((0, 0, 3, 1), (1, 0, 3, 1), (6, 2, 1, 3), (5, 0, 3, 2), (3, 0, 3, 0)), 0),
            (1, 0, 1, 0, 15, ((5, 0, 15, 7), (1, 0, 15, 8), (3, 0, 15, 4)), 0),
            (1, 0, 2, 0, 7, ((6, 2, 2, 10), (5, 0, 7, 8), (3, 0, 7, 5)), 0),
            (5, 0, 21, 2, 2, ((0, 1, 15, 24),), 0),
            (2, 1, 5, 0, 13, ((3, 0, 13, 12),), 0),
            (3, 1, 13, 0, 1, ((7, 2, 3, 21), (6, 2, 5, 20), (3, 0, 1, 18)), 0),
            (3, 1, 14, 2, 1, ((0, 1, 12, 16),), 0),
            (2, 1, 6, 1, 14, ((4, 1, 14, 16),), 0),
            (2, 1, 7, 2, 0, ((1, 1, 14, 17),), 0),
            (2, 1, 8, 0, 11, ((2, 1, 11, 18), (3, 0, 11, 13)), 0),
            (3, 1, 15, 1, 12, ((4, 1, 12, 19),), 0),
            (2, 1, 9, 0, 5, ((9, 1, 5, 18), (0, 0, 5, 14), (3, 0, 5, 14)), 0),
            (3, 1, 16, 1, 11, ((4, 1, 11, 20),), 0),
            (3, 1, 17, 0, 9, ((3, 0, 9, 19),), 0),
        ),
        ((0, 0, 2), (3, 0, 14), (4, 0, 6), (10, 0, 4), (11, 0, 12), (12, 0, 10), (18, 0, 8), (19, 0, 0), (20, 1, 15), (22, 1, 9), (23, 1, 13), (24, 1, 10), (25, 1, 8)),
    ),
    (
        (
            (0, 0, -1, 0, 4, ((1, 0, 4, 2), (0, 0, 4, 1), (5, 0, 4, 3), (3, 0, 4, 0)), 0),
            (3, 0, 11, 0, 2, ((0, 0, 2, 20), (3, 0, 2, 11)), 0),
            (3, 0, 12, 0, 10, ((3, 0, 10, 12),), 0),
            (5, 0, 21, 2, 3, ((2, 1, 7, 22), (8, 2, 0, 21)), 0),
            (1, 0, 1, 0, 6, ((1, 0, 6, 11), (3, 0, 6, 4)), 0),
            (1, 0, 2, 2, 0, ((0, 1, 6, 8),), 0),
            (2, 0, 8, 2, 1, ((2, 1, 1, 13),), 0),
            (6, 0, 22, 1, 6, ((8, 1, 6, 24),), 0),
            (1, 0, 3, 0, 8, ((5, 0, 8, 12), (7, 2, 0, 7), (1, 0, 8, 12), (3, 0, 8, 5)), 0),
            (2, 1, 9, 2, 2, ((0, 1, 4, 16),), 0),
            (1, 1, 5, 0, 0, ((5, 0, 0, 13), (0, 0, 0, 13), (3, 0, 0, 6)), 0),
            (3, 1, 17, 0, 14, ((3, 0, 14, 17),), 0),
            (3, 1, 18, 1, 0, ((2, 2, 1, 20),), 0),
            (2, 1, 10, 0, 12, ((3, 0, 12, 10),), 0),
        ),
        ((0, 0, 5), (4, 0, 7), (6, 0, 9), (7, 0, 1), (13, 0, 13), (14, 0, 3), (15, 0, 11), (16, 1, 1), (19, 1, 7), (20, 0, 15), (23, 1, 3), (24, 1, 5), (25, 1, 4), (26, 1, 2)),
    ),
    (
        (
            (0, 0, -1, 0, 5, ((5, 0, 5, 3), (1, 0, 5, 1), (0, 0, 5, 2), (3, 0, 5, 0)), 0),
            (1, 0, 1, 0, 7, ((3, 0, 7, 4),), 0),
            (4, 0, 16, 1, 8, ((2, 2, 0, 18), (8, 1, 8, 21)), 0),
            (5, 0, 18, 1, 11, ((4, 1, 11, 23),), 0),
            (5, 0, 19, 1, 10, ((8, 1, 10, 23),), 0),
            (1, 0, 2, 0, 9, ((5, 0, 9, 10), (3, 0, 9, 6)), 0),
            (5, 0, 20, 1, 13, ((8, 1, 13, 24),), 0),
            (1, 0, 3, 0, 1, ((7, 2, 0, 10), (5, 0, 1, 11), (3, 0, 1, 7)), 0),
            (5, 1, 21, 1, 12, ((4, 1, 12, 24),), 0),
            (2, 1, 7, 0, 13, ((3, 0, 13, 13),), 0),
            (3, 1, 13, 2, 0, ((8, 2, 1, 19), (2, 1, 11, 17)), 0),
            (3, 1, 14, 1, 9, ((4, 1, 9, 20),), 0),
            (2, 1, 8, 0, 3, ((3, 0, 3, 14),), 0),
            (6, 1, 23, 1, 14, ((4, 1, 14, 25),), 0),
            (2, 1, 9, 0, 11, ((3, 0, 11, 15),), 0),
            (3, 1, 15, 0, 15, ((3, 0, 15, 20),), 0),
        ),
        ((0, 0, 4), (4, 0, 6), (5, 0, 8), (6, 0, 0), (10, 0, 12), (11, 0, 2), (12, 0, 10), (17, 0, 14), (22, 1, 15)),
    ),
    (
        (
            (0, 0, -1, 0, 6, ((1, 0, 6, 3), (0, 0, 6, 2), (5, 0, 6, 1), (3, 0, 6, 0)), 0),
            (4, 0, 16, 0, 12, ((3, 0, 12, 18),), 0),
            (3, 0, 12, 0, 8, ((1, 0, 8, 20), (3, 0, 8, 13)), 0),
            (3, 0, 13, 0, 0, ((0, 0, 0, 16), (1, 0, 0, 21), (3, 0, 0, 14)), 0),
            (6, 0, 21, 2, 0, ((2, 1, 5, 24), (5, 1, 5, 24)), 0),
            (1, 0, 1, 0, 2, ((3, 0, 2, 4),), 0),
            (6, 1, 22, 2, 1, ((5, 1, 2, 26),), 0),
            (1, 1, 2, 0, 10, ((9, 2, 0, 8), (3, 0, 10, 5)), 0),
            (1, 1, 3, 0, 4, ((3, 0, 4, 6),), 0),
            (2, 1, 8, 1, 2, ((8, 1, 2, 18), (2, 2, 0, 15)), 0),
            (2, 1, 10, 0, 14, ((3, 0, 14, 12),), 0),
        ),
        ((0, 0, 7), (4, 0, 3), (5, 0, 11), (6, 0, 5), (7, 1, 3), (9, 1, 5), (11, 0, 15), (14, 0, 9), (15, 0, 1), (17, 1, 7), (18, 0, 13), (19, 1, 1), (20, 1, 6), (23, 1, 0), (24, 1, 4)),
    ),
    (
        (
            (0, 0, -1, 0, 7, ((7, 2, 0, 1), (1, 0, 7, 2), (0, 0, 7, 3), (5, 0, 7, 1), (3, 0, 7, 0)), 0),
            (4, 0, 16, 0, 13, ((3, 0, 13, 18),), 0),
            (4, 0, 17, 1, 14, ((8, 1, 14, 21),), 0),
            (1, 0, 1, 0, 3, ((0, 0, 3, 11), (3, 0, 3, 4)), 0),
            (5, 0, 20, 1, 13, ((8, 1, 13, 22),), 0),
            (1, 0, 2, 0, 11, ((1, 0, 11, 8), (3, 0, 11, 5)), 0),
            (2, 0, 7, 1, 11, ((5, 2, 0, 13), (8, 1, 11, 14)), 0),
            (1, 0, 3, 0, 5, ((1, 0, 5, 9), (0, 0, 5, 13), (3, 0, 5, 6)), 0),
            (5, 0, 22, 1, 12, ((8, 1, 12, 23),), 0),
            (2, 1, 8, 0, 15, ((5, 0, 15, 15), (3, 0, 15, 11)), 0),
            (2, 1, 9, 2, 0, ((4, 2, 0, 13),), 0),
            (2, 1, 10, 0, 9, ((2, 2, 1, 14), (3, 0, 9, 14)), 0),
            (2, 1, 11, 0, 1, ((3, 0, 1, 15),), 0),
            (3, 1, 15, 1, 9, ((8, 1, 9, 18),), 0),
            (4, 1, 19, 2, 1, ((2, 1, 9, 19),), 0),
        ),
        ((0, 0, 6), (4, 0, 2), (5, 0, 10), (6, 0, 4), (12, 0, 14), (13, 0, 8), (14, 0, 0), (18, 0, 12), (21, 1, 10), (23, 1, 8), (24, 1, 15)),
    ),
    (
        (
            (0, 0, -1, 0, 8, ((0, 0, 8, 3), (5, 0, 8, 3), (1, 0, 8, 3), (3, 0, 8, 0)), 0),
            (4, 0, 17, 2, 1, ((2, 2, 2, 21),), 0),
            (4, 0, 18, 1, 2, ((4, 1, 2, 19),), 0),
            (4, 0, 19, 1, 3, ((4, 1, 3, 20),), 0),
            (4, 0, 20, 0, 2, ((3, 0, 2, 19),), 0),
            (2, 0, 7, 2, 0, ((2, 2, 1, 14),), 0),
            (1, 0, 1, 0, 4, ((5, 0, 4, 9), (3, 0, 4, 5)), 0),
            (5, 0, 22, 1, 0, ((8, 1, 0, 19), (4, 1, 0, 21)), 0),
            (1, 1, 2, 0, 12, ((3, 0, 12, 6),), 0),
            (2, 1, 8, 1, 6, ((8, 1, 6, 14), (4, 1, 6, 15)), 0),
            (2, 1, 9, 0, 14, ((0, 0, 14, 17), (3, 0, 14, 12)), 0),
            (1, 1, 3, 0, 10, ((1, 0, 10, 9), (0, 0, 10, 12), (3, 0, 10, 7)), 0),
            (2, 1, 10, 1, 7, ((4, 1, 7, 14), (8, 1, 7, 13)), 0),
            (5, 1, 23, 1, 1, ((8, 1, 1, 20), (4, 1, 1, 22)), 0),
            (2, 1, 12, 0, 6, ((1, 0, 6, 13), (3, 0, 6, 13)), 0),
            (2, 1, 13, 0, 0, ((3, 0, 0, 14),), 0),
        ),
        ((0, 0, 9), (4, 0, 5), (5, 0, 13), (6, 0, 11), (11, 0, 15), (14, 0, 1), (15, 0, 7), (16, 1, 4), (21, 0, 3), (24, 1, 5)),
    ),
    (
        (
            (0, 0, -1, 0, 9, ((0, 0, 9, 2), (1, 0, 9, 2), (5, 0, 9, 4), (3, 0, 9, 0)), 0),
            (4, 0, 18, 1, 12, ((8, 1, 12, 22),), 0),
            (1, 0, 1, 1, 11, ((8, 1, 11, 9),), 0),
            (1, 0, 2, 0, 5, ((1, 0, 5, 6), (3, 0, 5, 4)), 0),
            (2, 0, 8, 0, 15, ((3, 0, 15, 11),), 0),
            (1, 0, 3, 0, 13, ((5, 0, 13, 12), (0, 0, 13, 7), (3, 0, 13, 5)), 0),
            (1, 0, 4, 0, 11, ((1, 0, 11, 8), (0, 0, 11, 9), (3, 0, 11, 6)), 0),
            (2, 0, 9, 2, 0, ((2, 1, 11, 15), (5, 1, 11, 19)), 0),
            (2, 0, 10, 0, 1, ((3, 0, 1, 14),), 0),
            (6, 0, 22, 2, 1, ((2, 1, 15, 23),), 0),
            (2, 0, 11, 0, 7, ((3, 0, 7, 15),), 0),
            (3, 1, 17, 0, 3, ((3, 0, 3, 21),), 0),
        ),
        ((0, 0, 8), (5, 0, 4), (6, 0, 12), (7, 0, 10), (12, 0, 14), (13, 0, 6), (14, 0, 0), (15, 1, 10), (16, 1, 13), (19, 0, 2), (20, 1, 14), (21, 1, 15), (23, 1, 8), (24, 1, 9)),
    ),
    (
        (
            (0, 0, -1, 0, 10, ((0, 0, 10, 2), (1, 0, 10, 3), (5, 0, 10, 3), (3, 0, 10, 0)), 0),
            (7, 0, 20, 1, 3, ((4, 1, 3, 24),), 0),
            (5, 0, 17, 1, 7, ((8, 1, 7, 24),), 0),
            (1, 0, 1, 0, 14, ((3, 0, 14, 6),), 0),
            (1, 0, 2, 0, 6, ((5, 0, 6, 12), (1, 0, 6, 10), (3, 0, 6, 8)), 0),
            (1, 0, 3, 0, 8, ((1, 0, 8, 9), (3, 0, 8, 7)), 0),
            (4, 0, 16, 0, 0, ((3, 0, 0, 21),), 0),
            (5, 0, 18, 2, 0, ((0, 1, 0, 23),), 0),
            (2, 1, 7, 0, 2, ((3, 0, 2, 14),), 0),
            (2, 1, 8, 0, 12, ((0, 0, 12, 16), (3, 0, 12, 15)), 0),
            (2, 1, 9, 0, 4, ((3, 0, 4, 16),), 0),
            (6, 1, 19, 1, 2, ((4, 1, 2, 23),), 0),
            (3, 1, 14, 1, 4, ((4, 1, 4, 17),), 0),
        ),
        ((0, 0, 11), (4, 0, 15), (5, 0, 9), (6, 0, 7), (10, 0, 3), (11, 0, 13), (12, 0, 5), (13, 1, 5), (15, 0, 1), (21, 1, 6), (22, 1, 0), (23, 1, 1)),
    ),
    (
        (
            (0, 0, -1, 0, 11, ((0, 0, 11, 2), (5, 0, 11, 4), (1, 0, 11, 3), (3, 0, 11, 0)), 0),
            (1, 0, 1, 0, 15, ((5, 0, 15, 8), (3, 0, 15, 4)), 0),
            (1, 0, 2, 2, 0, ((0, 1, 11, 7),), 0),
            (1, 0, 3, 0, 7, ((1, 0, 7, 8), (5, 0, 7, 11), (3, 0, 7, 6)), 0),
            (1, 0, 4, 0, 9, ((1, 0, 9, 9), (3, 0, 9, 5)), 0),
            (1, 0, 5, 2, 1, ((8, 2, 0, 9),), 0),
            (5, 0, 22, 1, 14, ((4, 1, 14, 23),), 0),
            (2, 0, 9, 1, 9, ((4, 1, 9, 12), (2, 2, 4, 17)), 0),
            (2, 0, 10, 1, 8, ((8, 1, 8, 15),), 0),
            (2, 1, 11, 0, 3, ((5, 0, 3, 17), (3, 0, 3, 10)), 0),
            (2, 1, 12, 0, 13, ((0, 0, 13, 16), (3, 0, 13, 11)), 0),
            (3, 1, 17, 0, 1, ((3, 0, 1, 15),), 0),
            (3, 1, 18, 1, 12, ((8, 1, 12, 20),), 0),
            (2, 1, 13, 0, 5, ((3, 0, 5, 12),), 0),
            (3, 1, 20, 1, 13, ((4, 1, 13, 20), (8, 1, 13, 21)), 0),
        ),
        ((0, 0, 10), (6, 0, 14), (7, 0, 8), (8, 0, 6), (14, 0, 2), (15, 0, 12), (16, 0, 4), (19, 1, 11), (21, 0, 0), (23, 1, 10), (24, 1, 15)),
    ),
    (
        (
            (0, 0, -1, 0, 12, ((0, 0, 12, 5), (5, 0, 12, 2), (1, 0, 12, 2), (3, 0, 12, 0)), 0),
            (4, 0, 13, 0, 6, ((4, 2, 0, 18), (3, 0, 6, 16)), 0),
            (1, 0, 1, 0, 14, ((0, 0, 14, 9), (1, 0, 14, 9), (3, 0, 14, 3)), 0),
            (4, 0, 14, 2, 1, ((1, 1, 0, 22),), 0),
            (6, 0, 19, 1, 0, ((4, 1, 0, 21),), 0),
            (1, 0, 2, 0, 0, ((5, 0, 0, 7), (2, 2, 0, 9), (3, 0, 0, 4)), 0),
            (1, 0, 3, 0, 8, ((3, 0, 8, 5),), 0),
            (2, 1, 6, 0, 4, ((3, 0, 4, 9),), 0),
            (2, 1, 7, 0, 2, ((3, 0, 2, 10),), 0),
            (6, 1, 20, 1, 1, ((8, 1, 1, 23),), 0),
            (6, 1, 21, 1, 6, ((4, 1, 6, 22),), 0),
            (6, 1, 22, 1, 7, ((4, 1, 7, 23),), 0),
            (2, 1, 8, 2, 0, ((1, 1, 3, 19),), 0),
            (2, 1, 9, 0, 10, ((3, 0, 10, 11),), 0),
        ),
        ((0, 0, 13), (4, 0, 1), (5, 0, 9), (10, 0, 5), (11, 0, 3), (12, 0, 11), (15, 0, 15), (16, 0, 7), (17, 1, 2), (18, 1, 3), (23, 1, 4), (24, 1, 5)),
    ),
    (
        (
            (0, 0, -1, 0, 13, ((4, 2, 0, 2), (1, 0, 13, 3), (5, 0, 13, 2), (0, 0, 13, 3), (3, 0, 13, 0)), 0),
            (5, 0, 19, 2, 2, ((8, 2, 3, 23), (2, 1, 15, 20)), 0),
            (1, 0, 1, 0, 1, ((5, 0, 1, 7), (1, 0, 1, 10), (3, 0, 1, 4)), 0),
            (5, 0, 20, 1, 11, ((2, 2, 1, 22), (8, 1, 11, 25)), 0),
            (1, 0, 2, 0, 9, ((0, 0, 9, 9), (3, 0, 9, 5)), 0),
            (6, 0, 22, 1, 9, ((4, 1, 9, 24),), 0),
            (2, 1, 6, 0, 5, ((3, 0, 5, 10),), 0),
            (2, 1, 7, 0, 3, ((3, 0, 3, 11),), 0),
            (6, 1, 23, 1, 8, ((8, 1, 8, 26),), 0),
            (3, 1, 12, 1, 15, ((5, 2, 0, 18), (8, 1, 15, 17)), 0),
            (2, 1, 8, 0, 11, ((0, 0, 11, 15), (3, 0, 11, 12)), 0),
            (3, 1, 13, 0, 15, ((3, 0, 15, 15),), 0),
            (3, 1, 14, 0, 7, ((3, 0, 7, 16),), 0),
            (4, 1, 17, 2, 1, ((8, 2, 2, 21), (2, 1, 8, 19)), 0),
            (3, 1, 15, 2, 0, ((5, 1, 11, 19),), 0),
        ),
        ((0, 0, 12), (3, 0, 14), (4, 0, 0), (5, 0, 8), (9, 0, 4), (10, 0, 2), (11, 0, 10), (16, 0, 6), (18, 1, 10), (21, 1, 14), (24, 1, 12), (25, 1, 13)),
    ),
    (
        (
            (0, 0, -1, 0, 14, ((5, 0, 14, 1), (0, 0, 14, 1), (1, 0, 14, 1), (3, 0, 14, 0)), 0),
            (1, 0, 1, 0, 2, ((1, 0, 2, 7), (5, 0, 2, 7), (3, 0, 2, 4)), 0),
            (5, 0, 18, 2, 0, ((5, 1, 1, 20),), 0),
            (1, 0, 2, 0, 12, ((0, 0, 12, 8), (1, 0, 12, 8), (3, 0, 12, 5)), 0),
            (5, 1, 19, 1, 4, ((8, 1, 4, 21),), 0),
            (1, 1, 3, 0, 10, ((0, 0, 10, 11), (3, 0, 10, 6)), 0),
            (5, 1, 20, 1, 5, ((8, 1, 5, 22),), 0),
            (2, 1, 7, 0, 0, ((4, 2, 1, 17), (3, 0, 0, 10)), 0),
            (3, 1, 13, 0, 4, ((3, 0, 4, 15),), 0),
            (3, 1, 14, 1, 1, ((8, 1, 1, 18),), 0),
            (2, 1, 9, 0, 8, ((3, 0, 8, 11),), 0),
            (2, 1, 10, 0, 6, ((3, 0, 6, 12),), 0),
        ),
        ((0, 0, 15), (4, 0, 3), (5, 0, 13), (6, 0, 11), (8, 0, 1), (11, 0, 7), (12, 0, 9), (15, 1, 0), (16, 0, 5), (17, 1, 2), (21, 1, 6), (22, 1, 7), (23, 1, 3)),
    ),
    (
        (
            (0, 0, -1, 0, 15, ((0, 0, 15, 1), (2, 2, 0, 2), (1, 0, 15, 1), (3, 0, 15, 0)), 0),
            (5, 0, 16, 1, 12, ((8, 1, 12, 21),), 0),
            (4, 0, 14, 0, 5, ((3, 0, 5, 16),), 0),
            (5, 0, 18, 2, 0, ((2, 1, 15, 22),), 0),
            (1, 0, 1, 0, 3, ((7, 2, 0, 7), (3, 0, 3, 4)), 0),
            (5, 0, 20, 2, 1, ((4, 2, 1, 22), (5, 1, 9, 22)), 0),
            (6, 0, 21, 2, 2, ((2, 1, 10, 23),), 0),
            (1, 0, 2, 0, 13, ((2, 2, 2, 9), (3, 0, 13, 5)), 0),
            (6, 0, 22, 1, 14, ((4, 1, 14, 23),), 0),
            (1, 0, 3, 0, 11, ((3, 0, 11, 6),), 0),
            (6, 0, 23, 2, 3, ((2, 1, 13, 25),), 0),
            (2, 0, 7, 0, 1, ((0, 0, 1, 13), (1, 0, 1, 17), (3, 0, 1, 8)), 0),
            (2, 1, 8, 0, 7, ((5, 0, 7, 14), (3, 0, 7, 11)), 0),
            (6, 1, 24, 1, 15, ((4, 1, 15, 24), (8, 1, 15, 25)), 0),
            (2, 1, 9, 0, 9, ((0, 0, 9, 17), (3, 0, 9, 12)), 0),
            (3, 1, 13, 1, 8, ((5, 2, 1, 17), (8, 1, 8, 18)), 0),
        ),
        ((0, 0, 14), (4, 0, 2), (5, 0, 12), (6, 0, 10), (10, 0, 0), (11, 0, 8), (12, 0, 6), (15, 0, 4), (17, 1, 13), (19, 1, 11), (25, 1, 9), (26, 1, 10)),
    ),
)
VMEM_LIMIT = 27 << 20
MBV, NBV = 512, 1024
LAST = 2

F32, BF16 = jnp.float32, jnp.bfloat16
MESH = pl.DeviceIdType.MESH
NT_PTS = 3
PAIRS, ROWS, COLS, OWN = 2048, 2048, 1024, 128
KC = PAIRS // NC
KK = 512
NK = PAIRS // KK
PER = KK // KC
MB, NB = MBV, NBV
NM = ROWS // MB
MB2 = 512
NM2 = ROWS // MB2
EARLY = NK - LAST
START = SMAX + PER
STEPS = NC + SMAX


def flip(value, bits):
    return [jnp.int32(b) * (1 - 2 * ((value // b) % 2)) for b in bits]


def flipped(value, deltas, bits, mask):
    for delta, bit in zip(deltas, bits):
        if mask & bit:
            value = value + delta
    return value


def weigh(x, factor, w_ref):
    rows, x = x.shape[0], x.astype(F32)
    for t in range(NT_PTS):
        w_ref[pl.ds(t * rows, rows), :] = (x * factor(t)).astype(BF16)


def product(w, y):
    return lax.dot_general(w, y, (((1,), (1,)), ((), ())), preferred_element_type=F32)


def gather_kernel(points, weights, own_ref, den_ref, acc, x_ref, y_ref, f_ref,
                  transit, w_ref, send_sem, recv_sem, local_sem):
    row, col = lax.axis_index("row"), lax.axis_index("col")
    row_d, col_d = flip(row, (1, 2, 4)), flip(col, (1, 2, 4, 8))
    peers = [
        {"row": flipped(row, row_d, (1, 2, 4), dr), "col": flipped(col, col_d, (1, 2, 4, 8), dc)}
        for dr, dc in TARGETS
    ]
    barrier = pltpu.get_barrier_semaphore()
    for peer in peers:
        pl.semaphore_signal(barrier, inc=1, device_id=peer, device_id_type=MESH)

    high = row // 4
    code = row * 2 + high
    code_d = flip(code, (1, 2, 4, 8))

    def lanes(j):
        return pl.ds(pl.multiple_of((j % PER) * KC, KC), KC)

    def place(kind, mark, j):
        if kind == 2:
            return transit.at[j, mark]
        slot = flipped(code, code_d, (1, 2, 4, 8), mark)
        if kind == 0:
            return x_ref.at[j // PER, pl.ds(pl.multiple_of(slot * OWN, OWN), OWN), lanes(j)]
        slot = slot % 8
        return y_ref.at[j // PER, pl.ds(pl.multiple_of(slot * OWN, OWN), OWN), lanes(j)]

    for k in range(NK):
        x_ref[k, pl.ds(pl.multiple_of(col * OWN, OWN), OWN), :] = own_ref[pl.ds(k * KK, KK), :].T
    for t in range(NT_PTS):
        f_ref[t, :] = weights[t] * jnp.exp(-points[t] * den_ref[...])
    pl.semaphore_wait(barrier, len(TARGETS))

    k_col = col // 2
    bits = [((row // b) % 2 + (k_col // b) % 2) % 2 for b in (4, 2, 1)]
    which = (bits[0] * 4 + bits[1] * 2 + bits[2]) * 2 + ((col % 2) + high) % 2

    def arrived(kind, mark, event, j):
        ref = place(kind, mark, j)
        pltpu.make_async_copy(ref, ref, recv_sem.at[j, event]).wait()

    def act(action, j):
        _, _, event, kind, mark, kids, local = action
        if event >= 0:
            arrived(kind, mark, event, j)
        src = place(kind, mark, j)
        for target, to_kind, to_mark, to_event in kids:
            pltpu.make_async_remote_copy(
                src_ref=src, dst_ref=place(to_kind, to_mark, j),
                send_sem=send_sem.at[j], recv_sem=recv_sem.at[j, to_event],
                device_id=peers[target], device_id_type=MESH,
            ).start()
        if local:
            pltpu.make_async_copy(src, place(1, mark, j), local_sem.at[j]).start()

    def bulk_wait(sem, copies):
        ref = acc.at[0, pl.ds(0, copies * OWN * KC // (2 * COLS)), :]
        pltpu.make_async_copy(ref, ref, sem).wait()

    def choose(run, low, high):
        if high - low == 1:
            run(low)
            return
        middle = (low + high) // 2
        pl.when(which < middle)(lambda: choose(run, low, middle))
        pl.when(which >= middle)(lambda: choose(run, middle, high))

    def settle(j):
        def run(g):
            actions, last = PROGRAMS[g]
            for event, kind, mark in last:
                arrived(kind, mark, event, j)
            copies = sum(a[6] for a in actions)
            if copies:
                bulk_wait(local_sem.at[j], copies)

        choose(run, 0, len(PROGRAMS))

    def block(k, m):
        rows = pl.ds(pl.multiple_of(m * MB, MB), MB)
        weigh(x_ref[k, rows, :], lambda t: f_ref[pl.ds(t, 1), pl.ds(pl.multiple_of(k * KK, KK), KK)], w_ref)

        @pl.loop(0, COLS // NB)
        def _(n):
            at = pl.ds(pl.multiple_of(n * NB, NB), NB)
            for t in range(NT_PTS):
                acc[t, rows, at] += product(w_ref[pl.ds(t * MB, MB), :], y_ref[k, at, :])

    @pl.loop(0, STEPS)
    def _(p):
        k = jnp.maximum(p - START, 0) // PER
        part = jnp.maximum(p - START, 0) % PER
        busy = jnp.logical_and(p >= START, p < START + EARLY * PER)

        @pl.when(jnp.logical_and(busy, part == 0))
        def _():
            for i in range(PER):
                settle(k * PER + i)

        @pl.loop(0, NG)
        def _(group):
            def run(g):
                for at in range(NG):
                    mine = [a for a in PROGRAMS[g][0] if a[1] == at]

                    def go(mine=mine):
                        for lag, same in itertools.groupby(mine, lambda a: a[0]):
                            @pl.when(jnp.logical_and(p >= lag, p < NC + lag))
                            def _(lag=lag, same=tuple(same)):
                                for a in same:
                                    act(a, p - lag)
                    if NG > 1:
                        pl.when(group == at)(go)
                    else:
                        go()

            choose(run, 0, len(PROGRAMS))

            if not EARLY:
                return

            @pl.when(jnp.logical_and(p == 0, group == 0))
            def _():
                @pl.loop(0, ROWS // 64)
                def _(m):
                    at = pl.ds(pl.multiple_of(m * 64, 64), 64)
                    acc[:, at, :] = jnp.zeros((NT_PTS, 64, COLS), F32)

            @pl.when(busy)
            def _():
                for b in range(NM // PER // NG):
                    block(k, (part * NG + group) * (NM // PER // NG) + b)

    @pl.loop(NC - PER * LAST, NC)
    def _(j):
        settle(j)

    def sent(g):
        @pl.loop(0, NC)
        def _(j):
            bulk_wait(send_sem.at[j], sum(len(a[5]) for a in PROGRAMS[g][0]))

    choose(sent, 0, len(PROGRAMS))


def last_kernel(acc, x_ref, y_ref, f_ref, out, w_ref, buf, sem):
    def copy(m, slot):
        return pltpu.make_async_copy(
            buf.at[slot], out.at[:, pl.ds(pl.multiple_of(m * MB2, MB2), MB2), :], sem.at[slot]
        )

    @pl.loop(0, NM2)
    def _(m):
        slot = m % 2
        rows = pl.ds(pl.multiple_of(m * MB2, MB2), MB2)

        @pl.when(m >= 2)
        def _():
            copy(m - 2, slot).wait()

        for k in range(EARLY, NK):
            at = slice(k * KK, (k + 1) * KK)
            weigh(x_ref[k, rows, :], lambda t: f_ref[t:t + 1, at], w_ref)
            for t in range(NT_PTS):
                d = product(w_ref[pl.ds(t * MB2, MB2), :], y_ref[k])
                if k > EARLY:
                    d += buf[slot, t]
                elif EARLY:
                    d += acc[t, rows, :]
                buf[slot, t] = d
        copy(m, slot).start()

    copy(NM2 - 2, (NM2 - 2) % 2).wait()
    copy(NM2 - 1, (NM2 - 1) % 2).wait()


def on_device(pair_ints, denominators, lap_points, lap_weights):
    vmem = pl.BlockSpec(memory_space=pltpu.VMEM)
    smem = pl.BlockSpec(memory_space=pltpu.SMEM)
    held = pl.pallas_call(
        gather_kernel,
        out_shape=(
            pltpu.VMEM((NT_PTS, ROWS, COLS), F32),
            pltpu.VMEM((NK, ROWS, KK), BF16),
            pltpu.VMEM((NK, COLS, KK), BF16),
            pltpu.VMEM((NT_PTS, PAIRS), F32),
        ),
        in_specs=[smem, smem, vmem, vmem],
        out_specs=(vmem,) * 4,
        scratch_shapes=[
            pltpu.VMEM((NC, NT, OWN, KC), BF16),
            pltpu.VMEM((NT_PTS * MB, KK), BF16),
            pltpu.SemaphoreType.DMA((NC,)),
            pltpu.SemaphoreType.DMA((NC, NE)),
            pltpu.SemaphoreType.DMA((NC,)),
        ],
        compiler_params=pltpu.CompilerParams(
            collective_id=0, has_side_effects=True, vmem_limit_bytes=VMEM_LIMIT
        ),
    )(lap_points, lap_weights, pair_ints, denominators)
    held = [pltpu.with_memory_space_constraint(a, pltpu.VMEM) for a in held]
    return pl.pallas_call(
        last_kernel,
        out_shape=jax.ShapeDtypeStruct((NT_PTS, ROWS, COLS), F32),
        in_specs=[vmem] * 4,
        out_specs=pl.BlockSpec(memory_space=pl.ANY),
        scratch_shapes=[
            pltpu.VMEM((NT_PTS * MB2, KK), BF16),
            pltpu.VMEM((2, NT_PTS, MB2, COLS), F32),
            pltpu.SemaphoreType.DMA((2,)),
        ],
        compiler_params=pltpu.CompilerParams(vmem_limit_bytes=VMEM_LIMIT),
    )(*held)


def solution(mesh):
    in_specs = (P(None, ("row", "col")), P(), P(), P())
    out_specs = P(None, "row", "col")
    return jax.shard_map(
        on_device, mesh=mesh, in_specs=in_specs, out_specs=out_specs, check_vma=False
    )
```

```python
import itertools

import jax
import jax.numpy as jnp
from jax import lax
from jax.experimental import pallas as pl
from jax.experimental.pallas import tpu as pltpu
from jax.sharding import PartitionSpec as P

NC, NG, SMAX, NT, NE = 8, 1, 8, 6, 27
TARGETS = ((0, 12), (0, 4), (4, 2), (0, 1), (3, 0), (0, 2), (1, 1), (3, 1), (1, 0), (4, 3))
PROGRAMS = (
    (
        (
            (0, 0, -1, 0, 0, ((0, 0, 0, 2), (1, 0, 0, 5), (2, 2, 1, 5), (3, 0, 0, 0)), 1),
            (1, 0, 1, 2, 0, ((1, 2, 1, 8),), 0),
            (4, 0, 18, 0, 10, ((7, 1, 10, 22), (3, 0, 10, 16)), 0),
            (3, 0, 15, 0, 7, (), 1),
            (1, 0, 2, 0, 4, ((4, 1, 4, 8), (5, 0, 4, 7), (0, 0, 4, 6), (3, 0, 4, 4)), 1),
            (1, 0, 3, 2, 1, ((2, 1, 1, 10), (5, 1, 1, 9)), 0),
            (2, 0, 9, 0, 14, ((6, 1, 14, 15), (3, 0, 14, 10)), 0),
            (1, 0, 4, 0, 2, ((1, 0, 2, 11), (3, 0, 2, 6)), 1),
            (2, 0, 10, 2, 2, ((2, 1, 5, 18), (5, 1, 5, 16)), 0),
            (1, 0, 5, 0, 12, ((6, 1, 12, 6), (1, 0, 12, 10), (3, 0, 12, 5)), 0),
            (0, 0, 0, 0, 1, (), 1),
            (2, 0, 11, 0, 6, ((3, 0, 6, 11),), 1),
            (1, 0, 6, 0, 5, (), 1),
            (2, 0, 12, 0, 8, ((3, 0, 8, 12),), 0),
            (3, 0, 17, 2, 4, ((5, 1, 0, 22),), 0),
            (2, 0, 13, 2, 3, ((2, 1, 4, 20), (5, 1, 4, 17)), 0),
            (1, 0, 8, 0, 3, (), 1),
            (4, 0, 20, 2, 5, ((2, 1, 3, 23),), 0),
        ),
        ((7, 0, 13), (14, 0, 15), (16, 0, 9), (19, 0, 11)),
    ),
    (
        (
            (0, 0, -1, 0, 1, ((0, 0, 1, 1), (1, 0, 1, 3), (6, 1, 1, 2), (3, 0, 1, 0)), 0),
            (1, 0, 1, 0, 5, ((6, 1, 5, 6), (7, 1, 5, 7), (3, 0, 5, 6)), 0),
            (3, 0, 12, 0, 8, (), 1),
            (1, 0, 2, 0, 3, ((1, 0, 3, 8), (0, 0, 3, 7), (7, 1, 3, 9), (3, 0, 3, 8)), 0),
            (1, 0, 3, 0, 13, ((5, 0, 13, 5), (3, 0, 13, 7)), 1),
            (2, 0, 7, 0, 15, ((4, 1, 15, 15), (0, 0, 15, 13), (3, 0, 15, 14)), 1),
            (4, 0, 16, 0, 10, (), 1),
            (2, 0, 8, 0, 7, ((3, 0, 7, 15),), 0),
            (2, 0, 9, 0, 9, ((8, 1, 9, 16), (3, 0, 9, 16)), 1),
            (3, 0, 13, 2, 0, ((0, 2, 2, 19),), 0),
            (3, 0, 14, 2, 1, ((2, 1, 14, 17),), 0),
            (2, 0, 10, 0, 14, (), 1),
            (1, 0, 5, 0, 12, (), 1),
            (3, 0, 15, 0, 11, ((4, 1, 11, 20), (8, 1, 11, 22), (3, 0, 11, 19)), 1),
        ),
        ((0, 0, 0), (4, 0, 4), (6, 0, 2), (11, 0, 6)),
    ),
    (
        (
            (0, 0, -1, 0, 2, ((2, 1, 2, 1), (5, 0, 2, 4), (0, 0, 2, 1), (1, 0, 2, 1), (3, 0, 2, 0)), 0),
            (2, 0, 6, 1, 7, ((4, 1, 7, 16),), 0),
            (1, 0, 1, 0, 14, ((9, 1, 14, 10), (1, 0, 14, 10), (3, 0, 14, 3)), 0),
            (1, 0, 3, 0, 6, ((8, 2, 3, 13), (3, 0, 6, 4)), 0),
            (4, 0, 20, 0, 8, ((9, 1, 8, 23), (3, 0, 8, 18)), 0),
            (4, 0, 21, 0, 0, ((3, 0, 0, 19),), 0),
            (2, 0, 7, 0, 4, ((0, 0, 4, 13), (2, 1, 4, 16), (3, 0, 4, 10)), 0),
            (2, 0, 8, 0, 12, ((6, 2, 1, 14), (3, 0, 12, 11)), 0),
            (2, 0, 9, 1, 1, ((4, 1, 1, 19),), 0),
            (2, 0, 10, 2, 0, ((1, 1, 7, 17),), 0),
            (2, 0, 11, 0, 10, ((5, 0, 10, 18), (3, 0, 10, 12)), 0),
        ),
        ((0, 0, 3), (2, 1, 3), (4, 0, 15), (5, 0, 7), (12, 0, 13), (13, 0, 11), (14, 0, 5), (15, 1, 2), (16, 1, 5), (17, 1, 4), (18, 0, 1), (19, 0, 9), (22, 1, 0), (23, 1, 6)),
    ),
    (
        (
            (0, 0, -1, 0, 3, ((0, 0, 3, 1), (1, 0, 3, 1), (6, 2, 1, 3), (5, 0, 3, 2), (3, 0, 3, 0)), 0),
            (1, 0, 1, 0, 15, ((5, 0, 15, 7), (1, 0, 15, 8), (3, 0, 15, 4)), 0),
            (1, 0, 2, 0, 7, ((6, 2, 2, 10), (5, 0, 7, 8), (3, 0, 7, 5)), 0),
            (5, 0, 21, 2, 2, ((0, 1, 15, 24),), 0),
            (2, 0, 5, 0, 13, ((3, 0, 13, 12),), 0),
            (3, 0, 13, 0, 1, ((7, 2, 3, 21), (6, 2, 5, 20), (3, 0, 1, 18)), 0),
            (3, 0, 14, 2, 1, ((0, 1, 12, 16),), 0),
            (2, 0, 6, 1, 14, ((4, 1, 14, 16),), 0),
            (2, 0, 7, 2, 0, ((1, 1, 14, 17),), 0),
            (2, 0, 8, 0, 11, ((2, 1, 11, 18), (3, 0, 11, 13)), 0),
            (3, 0, 15, 1, 12, ((4, 1, 12, 19),), 0),
            (2, 0, 9, 0, 5, ((9, 1, 5, 18), (0, 0, 5, 14), (3, 0, 5, 14)), 0),
            (3, 0, 16, 1, 11, ((4, 1, 11, 20),), 0),
            (3, 0, 17, 0, 9, ((3, 0, 9, 19),), 0),
        ),
        ((0, 0, 2), (3, 0, 14), (4, 0, 6), (10, 0, 4), (11, 0, 12), (12, 0, 10), (18, 0, 8), (19, 0, 0), (20, 1, 15), (22, 1, 9), (23, 1, 13), (24, 1, 10), (25, 1, 8)),
    ),
    (
        (
            (0, 0, -1, 0, 4, ((1, 0, 4, 2), (0, 0, 4, 1), (5, 0, 4, 3), (3, 0, 4, 0)), 0),
            (3, 0, 11, 0, 2, ((0, 0, 2, 20), (3, 0, 2, 11)), 0),
            (3, 0, 12, 0, 10, ((3, 0, 10, 12),), 0),
            (5, 0, 21, 2, 3, ((2, 1, 7, 22), (8, 2, 0, 21)), 0),
            (1, 0, 1, 0, 6, ((1, 0, 6, 11), (3, 0, 6, 4)), 0),
            (1, 0, 2, 2, 0, ((0, 1, 6, 8),), 0),
            (2, 0, 8, 2, 1, ((2, 1, 1, 13),), 0),
            (6, 0, 22, 1, 6, ((8, 1, 6, 24),), 0),
            (1, 0, 3, 0, 8, ((5, 0, 8, 12), (7, 2, 0, 7), (1, 0, 8, 12), (3, 0, 8, 5)), 0),
            (2, 0, 9, 2, 2, ((0, 1, 4, 16),), 0),
            (1, 0, 5, 0, 0, ((5, 0, 0, 13), (0, 0, 0, 13), (3, 0, 0, 6)), 0),
            (3, 0, 17, 0, 14, ((3, 0, 14, 17),), 0),
            (3, 0, 18, 1, 0, ((2, 2, 1, 20),), 0),
            (2, 0, 10, 0, 12, ((3, 0, 12, 10),), 0),
        ),
        ((0, 0, 5), (4, 0, 7), (6, 0, 9), (7, 0, 1), (13, 0, 13), (14, 0, 3), (15, 0, 11), (16, 1, 1), (19, 1, 7), (20, 0, 15), (23, 1, 3), (24, 1, 5), (25, 1, 4), (26, 1, 2)),
    ),
    (
        (
            (0, 0, -1, 0, 5, ((5, 0, 5, 3), (1, 0, 5, 1), (0, 0, 5, 2), (3, 0, 5, 0)), 0),
            (1, 0, 1, 0, 7, ((3, 0, 7, 4),), 0),
            (4, 0, 16, 1, 8, ((2, 2, 0, 18), (8, 1, 8, 21)), 0),
            (5, 0, 18, 1, 11, ((4, 1, 11, 23),), 0),
            (5, 0, 19, 1, 10, ((8, 1, 10, 23),), 0),
            (1, 0, 2, 0, 9, ((5, 0, 9, 10), (3, 0, 9, 6)), 0),
            (5, 0, 20, 1, 13, ((8, 1, 13, 24),), 0),
            (1, 0, 3, 0, 1, ((7, 2, 0, 10), (5, 0, 1, 11), (3, 0, 1, 7)), 0),
            (5, 0, 21, 1, 12, ((4, 1, 12, 24),), 0),
            (2, 0, 7, 0, 13, ((3, 0, 13, 13),), 0),
            (3, 0, 13, 2, 0, ((8, 2, 1, 19), (2, 1, 11, 17)), 0),
            (3, 0, 14, 1, 9, ((4, 1, 9, 20),), 0),
            (2, 0, 8, 0, 3, ((3, 0, 3, 14),), 0),
            (6, 0, 23, 1, 14, ((4, 1, 14, 25),), 0),
            (2, 0, 9, 0, 11, ((3, 0, 11, 15),), 0),
            (3, 0, 15, 0, 15, ((3, 0, 15, 20),), 0),
        ),
        ((0, 0, 4), (4, 0, 6), (5, 0, 8), (6, 0, 0), (10, 0, 12), (11, 0, 2), (12, 0, 10), (17, 0, 14), (22, 1, 15)),
    ),
    (
        (
            (0, 0, -1, 0, 6, ((1, 0, 6, 3), (0, 0, 6, 2), (5, 0, 6, 1), (3, 0, 6, 0)), 0),
            (4, 0, 16, 0, 12, ((3, 0, 12, 18),), 0),
            (3, 0, 12, 0, 8, ((1, 0, 8, 20), (3, 0, 8, 13)), 0),
            (3, 0, 13, 0, 0, ((0, 0, 0, 16), (1, 0, 0, 21), (3, 0, 0, 14)), 0),
            (6, 0, 21, 2, 0, ((2, 1, 5, 24), (5, 1, 5, 24)), 0),
            (1, 0, 1, 0, 2, ((3, 0, 2, 4),), 0),
            (6, 0, 22, 2, 1, ((5, 1, 2, 26),), 0),
            (1, 0, 2, 0, 10, ((9, 2, 0, 8), (3, 0, 10, 5)), 0),
            (1, 0, 3, 0, 4, ((3, 0, 4, 6),), 0),
            (2, 0, 8, 1, 2, ((8, 1, 2, 18), (2, 2, 0, 15)), 0),
            (2, 0, 10, 0, 14, ((3, 0, 14, 12),), 0),
        ),
        ((0, 0, 7), (4, 0, 3), (5, 0, 11), (6, 0, 5), (7, 1, 3), (9, 1, 5), (11, 0, 15), (14, 0, 9), (15, 0, 1), (17, 1, 7), (18, 0, 13), (19, 1, 1), (20, 1, 6), (23, 1, 0), (24, 1, 4)),
    ),
    (
        (
            (0, 0, -1, 0, 7, ((7, 2, 0, 1), (1, 0, 7, 2), (0, 0, 7, 3), (5, 0, 7, 1), (3, 0, 7, 0)), 0),
            (4, 0, 16, 0, 13, ((3, 0, 13, 18),), 0),
            (4, 0, 17, 1, 14, ((8, 1, 14, 21),), 0),
            (1, 0, 1, 0, 3, ((0, 0, 3, 11), (3, 0, 3, 4)), 0),
            (5, 0, 20, 1, 13, ((8, 1, 13, 22),), 0),
            (1, 0, 2, 0, 11, ((1, 0, 11, 8), (3, 0, 11, 5)), 0),
            (2, 0, 7, 1, 11, ((5, 2, 0, 13), (8, 1, 11, 14)), 0),
            (1, 0, 3, 0, 5, ((1, 0, 5, 9), (0, 0, 5, 13), (3, 0, 5, 6)), 0),
            (5, 0, 22, 1, 12, ((8, 1, 12, 23),), 0),
            (2, 0, 8, 0, 15, ((5, 0, 15, 15), (3, 0, 15, 11)), 0),
            (2, 0, 9, 2, 0, ((4, 2, 0, 13),), 0),
            (2, 0, 10, 0, 9, ((2, 2, 1, 14), (3, 0, 9, 14)), 0),
            (2, 0, 11, 0, 1, ((3, 0, 1, 15),), 0),
            (3, 0, 15, 1, 9, ((8, 1, 9, 18),), 0),
            (4, 0, 19, 2, 1, ((2, 1, 9, 19),), 0),
        ),
        ((0, 0, 6), (4, 0, 2), (5, 0, 10), (6, 0, 4), (12, 0, 14), (13, 0, 8), (14, 0, 0), (18, 0, 12), (21, 1, 10), (23, 1, 8), (24, 1, 15)),
    ),
    (
        (
            (0, 0, -1, 0, 8, ((0, 0, 8, 3), (5, 0, 8, 3), (1, 0, 8, 3), (3, 0, 8, 0)), 0),
            (4, 0, 17, 2, 1, ((2, 2, 2, 21),), 0),
            (4, 0, 18, 1, 2, ((4, 1, 2, 19),), 0),
            (4, 0, 19, 1, 3, ((4, 1, 3, 20),), 0),
            (4, 0, 20, 0, 2, ((3, 0, 2, 19),), 0),
            (2, 0, 7, 2, 0, ((2, 2, 1, 14),), 0),
            (1, 0, 1, 0, 4, ((5, 0, 4, 9), (3, 0, 4, 5)), 0),
            (5, 0, 22, 1, 0, ((8, 1, 0, 19), (4, 1, 0, 21)), 0),
            (1, 0, 2, 0, 12, ((3, 0, 12, 6),), 0),
            (2, 0, 8, 1, 6, ((8, 1, 6, 14), (4, 1, 6, 15)), 0),
            (2, 0, 9, 0, 14, ((0, 0, 14, 17), (3, 0, 14, 12)), 0),
            (1, 0, 3, 0, 10, ((1, 0, 10, 9), (0, 0, 10, 12), (3, 0, 10, 7)), 0),
            (2, 0, 10, 1, 7, ((4, 1, 7, 14), (8, 1, 7, 13)), 0),
            (5, 0, 23, 1, 1, ((8, 1, 1, 20), (4, 1, 1, 22)), 0),
            (2, 0, 12, 0, 6, ((1, 0, 6, 13), (3, 0, 6, 13)), 0),
            (2, 0, 13, 0, 0, ((3, 0, 0, 14),), 0),
        ),
        ((0, 0, 9), (4, 0, 5), (5, 0, 13), (6, 0, 11), (11, 0, 15), (14, 0, 1), (15, 0, 7), (16, 1, 4), (21, 0, 3), (24, 1, 5)),
    ),
    (
        (
            (0, 0, -1, 0, 9, ((0, 0, 9, 2), (1, 0, 9, 2), (5, 0, 9, 4), (3, 0, 9, 0)), 0),
            (4, 0, 18, 1, 12, ((8, 1, 12, 22),), 0),
            (1, 0, 1, 1, 11, ((8, 1, 11, 9),), 0),
            (1, 0, 2, 0, 5, ((1, 0, 5, 6), (3, 0, 5, 4)), 0),
            (2, 0, 8, 0, 15, ((3, 0, 15, 11),), 0),
            (1, 0, 3, 0, 13, ((5, 0, 13, 12), (0, 0, 13, 7), (3, 0, 13, 5)), 0),
            (1, 0, 4, 0, 11, ((1, 0, 11, 8), (0, 0, 11, 9), (3, 0, 11, 6)), 0),
            (2, 0, 9, 2, 0, ((2, 1, 11, 15), (5, 1, 11, 19)), 0),
            (2, 0, 10, 0, 1, ((3, 0, 1, 14),), 0),
            (6, 0, 22, 2, 1, ((2, 1, 15, 23),), 0),
            (2, 0, 11, 0, 7, ((3, 0, 7, 15),), 0),
            (3, 0, 17, 0, 3, ((3, 0, 3, 21),), 0),
        ),
        ((0, 0, 8), (5, 0, 4), (6, 0, 12), (7, 0, 10), (12, 0, 14), (13, 0, 6), (14, 0, 0), (15, 1, 10), (16, 1, 13), (19, 0, 2), (20, 1, 14), (21, 1, 15), (23, 1, 8), (24, 1, 9)),
    ),
    (
        (
            (0, 0, -1, 0, 10, ((0, 0, 10, 2), (1, 0, 10, 3), (5, 0, 10, 3), (3, 0, 10, 0)), 0),
            (7, 0, 20, 1, 3, ((4, 1, 3, 24),), 0),
            (5, 0, 17, 1, 7, ((8, 1, 7, 24),), 0),
            (1, 0, 1, 0, 14, ((3, 0, 14, 6),), 0),
            (1, 0, 2, 0, 6, ((5, 0, 6, 12), (1, 0, 6, 10), (3, 0, 6, 8)), 0),
            (1, 0, 3, 0, 8, ((1, 0, 8, 9), (3, 0, 8, 7)), 0),
            (4, 0, 16, 0, 0, ((3, 0, 0, 21),), 0),
            (5, 0, 18, 2, 0, ((0, 1, 0, 23),), 0),
            (2, 0, 7, 0, 2, ((3, 0, 2, 14),), 0),
            (2, 0, 8, 0, 12, ((0, 0, 12, 16), (3, 0, 12, 15)), 0),
            (2, 0, 9, 0, 4, ((3, 0, 4, 16),), 0),
            (6, 0, 19, 1, 2, ((4, 1, 2, 23),), 0),
            (3, 0, 14, 1, 4, ((4, 1, 4, 17),), 0),
        ),
        ((0, 0, 11), (4, 0, 15), (5, 0, 9), (6, 0, 7), (10, 0, 3), (11, 0, 13), (12, 0, 5), (13, 1, 5), (15, 0, 1), (21, 1, 6), (22, 1, 0), (23, 1, 1)),
    ),
    (
        (
            (0, 0, -1, 0, 11, ((0, 0, 11, 2), (5, 0, 11, 4), (1, 0, 11, 3), (3, 0, 11, 0)), 0),
            (1, 0, 1, 0, 15, ((5, 0, 15, 8), (3, 0, 15, 4)), 0),
            (1, 0, 2, 2, 0, ((0, 1, 11, 7),), 0),
            (1, 0, 3, 0, 7, ((1, 0, 7, 8), (5, 0, 7, 11), (3, 0, 7, 6)), 0),
            (1, 0, 4, 0, 9, ((1, 0, 9, 9), (3, 0, 9, 5)), 0),
            (1, 0, 5, 2, 1, ((8, 2, 0, 9),), 0),
            (5, 0, 22, 1, 14, ((4, 1, 14, 23),), 0),
            (2, 0, 9, 1, 9, ((4, 1, 9, 12), (2, 2, 4, 17)), 0),
            (2, 0, 10, 1, 8, ((8, 1, 8, 15),), 0),
            (2, 0, 11, 0, 3, ((5, 0, 3, 17), (3, 0, 3, 10)), 0),
            (2, 0, 12, 0, 13, ((0, 0, 13, 16), (3, 0, 13, 11)), 0),
            (3, 0, 17, 0, 1, ((3, 0, 1, 15),), 0),
            (3, 0, 18, 1, 12, ((8, 1, 12, 20),), 0),
            (2, 0, 13, 0, 5, ((3, 0, 5, 12),), 0),
            (3, 0, 20, 1, 13, ((4, 1, 13, 20), (8, 1, 13, 21)), 0),
        ),
        ((0, 0, 10), (6, 0, 14), (7, 0, 8), (8, 0, 6), (14, 0, 2), (15, 0, 12), (16, 0, 4), (19, 1, 11), (21, 0, 0), (23, 1, 10), (24, 1, 15)),
    ),
    (
        (
            (0, 0, -1, 0, 12, ((0, 0, 12, 5), (5, 0, 12, 2), (1, 0, 12, 2), (3, 0, 12, 0)), 0),
            (4, 0, 13, 0, 6, ((4, 2, 0, 18), (3, 0, 6, 16)), 0),
            (1, 0, 1, 0, 14, ((0, 0, 14, 9), (1, 0, 14, 9), (3, 0, 14, 3)), 0),
            (4, 0, 14, 2, 1, ((1, 1, 0, 22),), 0),
            (6, 0, 19, 1, 0, ((4, 1, 0, 21),), 0),
            (1, 0, 2, 0, 0, ((5, 0, 0, 7), (2, 2, 0, 9), (3, 0, 0, 4)), 0),
            (1, 0, 3, 0, 8, ((3, 0, 8, 5),), 0),
            (2, 0, 6, 0, 4, ((3, 0, 4, 9),), 0),
            (2, 0, 7, 0, 2, ((3, 0, 2, 10),), 0),
            (6, 0, 20, 1, 1, ((8, 1, 1, 23),), 0),
            (6, 0, 21, 1, 6, ((4, 1, 6, 22),), 0),
            (6, 0, 22, 1, 7, ((4, 1, 7, 23),), 0),
            (2, 0, 8, 2, 0, ((1, 1, 3, 19),), 0),
            (2, 0, 9, 0, 10, ((3, 0, 10, 11),), 0),
        ),
        ((0, 0, 13), (4, 0, 1), (5, 0, 9), (10, 0, 5), (11, 0, 3), (12, 0, 11), (15, 0, 15), (16, 0, 7), (17, 1, 2), (18, 1, 3), (23, 1, 4), (24, 1, 5)),
    ),
    (
        (
            (0, 0, -1, 0, 13, ((4, 2, 0, 2), (1, 0, 13, 3), (5, 0, 13, 2), (0, 0, 13, 3), (3, 0, 13, 0)), 0),
            (5, 0, 19, 2, 2, ((8, 2, 3, 23), (2, 1, 15, 20)), 0),
            (1, 0, 1, 0, 1, ((5, 0, 1, 7), (1, 0, 1, 10), (3, 0, 1, 4)), 0),
            (5, 0, 20, 1, 11, ((2, 2, 1, 22), (8, 1, 11, 25)), 0),
            (1, 0, 2, 0, 9, ((0, 0, 9, 9), (3, 0, 9, 5)), 0),
            (6, 0, 22, 1, 9, ((4, 1, 9, 24),), 0),
            (2, 0, 6, 0, 5, ((3, 0, 5, 10),), 0),
            (2, 0, 7, 0, 3, ((3, 0, 3, 11),), 0),
            (6, 0, 23, 1, 8, ((8, 1, 8, 26),), 0),
            (3, 0, 12, 1, 15, ((5, 2, 0, 18), (8, 1, 15, 17)), 0),
            (2, 0, 8, 0, 11, ((0, 0, 11, 15), (3, 0, 11, 12)), 0),
            (3, 0, 13, 0, 15, ((3, 0, 15, 15),), 0),
            (3, 0, 14, 0, 7, ((3, 0, 7, 16),), 0),
            (4, 0, 17, 2, 1, ((8, 2, 2, 21), (2, 1, 8, 19)), 0),
            (3, 0, 15, 2, 0, ((5, 1, 11, 19),), 0),
        ),
        ((0, 0, 12), (3, 0, 14), (4, 0, 0), (5, 0, 8), (9, 0, 4), (10, 0, 2), (11, 0, 10), (16, 0, 6), (18, 1, 10), (21, 1, 14), (24, 1, 12), (25, 1, 13)),
    ),
    (
        (
            (0, 0, -1, 0, 14, ((5, 0, 14, 1), (0, 0, 14, 1), (1, 0, 14, 1), (3, 0, 14, 0)), 0),
            (1, 0, 1, 0, 2, ((1, 0, 2, 7), (5, 0, 2, 7), (3, 0, 2, 4)), 0),
            (5, 0, 18, 2, 0, ((5, 1, 1, 20),), 0),
            (1, 0, 2, 0, 12, ((0, 0, 12, 8), (1, 0, 12, 8), (3, 0, 12, 5)), 0),
            (5, 0, 19, 1, 4, ((8, 1, 4, 21),), 0),
            (1, 0, 3, 0, 10, ((0, 0, 10, 11), (3, 0, 10, 6)), 0),
            (5, 0, 20, 1, 5, ((8, 1, 5, 22),), 0),
            (2, 0, 7, 0, 0, ((4, 2, 1, 17), (3, 0, 0, 10)), 0),
            (3, 0, 13, 0, 4, ((3, 0, 4, 15),), 0),
            (3, 0, 14, 1, 1, ((8, 1, 1, 18),), 0),
            (2, 0, 9, 0, 8, ((3, 0, 8, 11),), 0),
            (2, 0, 10, 0, 6, ((3, 0, 6, 12),), 0),
        ),
        ((0, 0, 15), (4, 0, 3), (5, 0, 13), (6, 0, 11), (8, 0, 1), (11, 0, 7), (12, 0, 9), (15, 1, 0), (16, 0, 5), (17, 1, 2), (21, 1, 6), (22, 1, 7), (23, 1, 3)),
    ),
    (
        (
            (0, 0, -1, 0, 15, ((0, 0, 15, 1), (2, 2, 0, 2), (1, 0, 15, 1), (3, 0, 15, 0)), 0),
            (5, 0, 16, 1, 12, ((8, 1, 12, 21),), 0),
            (4, 0, 14, 0, 5, ((3, 0, 5, 16),), 0),
            (5, 0, 18, 2, 0, ((2, 1, 15, 22),), 0),
            (1, 0, 1, 0, 3, ((7, 2, 0, 7), (3, 0, 3, 4)), 0),
            (5, 0, 20, 2, 1, ((4, 2, 1, 22), (5, 1, 9, 22)), 0),
            (6, 0, 21, 2, 2, ((2, 1, 10, 23),), 0),
            (1, 0, 2, 0, 13, ((2, 2, 2, 9), (3, 0, 13, 5)), 0),
            (6, 0, 22, 1, 14, ((4, 1, 14, 23),), 0),
            (1, 0, 3, 0, 11, ((3, 0, 11, 6),), 0),
            (6, 0, 23, 2, 3, ((2, 1, 13, 25),), 0),
            (2, 0, 7, 0, 1, ((0, 0, 1, 13), (1, 0, 1, 17), (3, 0, 1, 8)), 0),
            (2, 0, 8, 0, 7, ((5, 0, 7, 14), (3, 0, 7, 11)), 0),
            (6, 0, 24, 1, 15, ((4, 1, 15, 24), (8, 1, 15, 25)), 0),
            (2, 0, 9, 0, 9, ((0, 0, 9, 17), (3, 0, 9, 12)), 0),
            (3, 0, 13, 1, 8, ((5, 2, 1, 17), (8, 1, 8, 18)), 0),
        ),
        ((0, 0, 14), (4, 0, 2), (5, 0, 12), (6, 0, 10), (10, 0, 0), (11, 0, 8), (12, 0, 6), (15, 0, 4), (17, 1, 13), (19, 1, 11), (25, 1, 9), (26, 1, 10)),
    ),
)
VMEM_LIMIT = 27 << 20
MBV, NBV = 512, 1024
LAST = 2

F32, BF16 = jnp.float32, jnp.bfloat16
MESH = pl.DeviceIdType.MESH
NT_PTS = 3
PAIRS, ROWS, COLS, OWN = 2048, 2048, 1024, 128
KC = PAIRS // NC
KK = 512
NK = PAIRS // KK
PER = KK // KC
MB, NB = MBV, NBV
NM = ROWS // MB
MB2 = 512
NM2 = ROWS // MB2
EARLY = NK - LAST
START = SMAX + PER - 1
STEPS = NC + SMAX


def flip(value, bits):
    return [jnp.int32(b) * (1 - 2 * ((value // b) % 2)) for b in bits]


def flipped(value, deltas, bits, mask):
    for delta, bit in zip(deltas, bits):
        if mask & bit:
            value = value + delta
    return value


def weigh(x, factor, w_ref):
    rows, x = x.shape[0], x.astype(F32)
    for t in range(NT_PTS):
        w_ref[pl.ds(t * rows, rows), :] = (x * factor(t)).astype(BF16)


def product(w, y):
    return lax.dot_general(w, y, (((1,), (1,)), ((), ())), preferred_element_type=F32)


def gather_kernel(points, weights, own_ref, den_ref, acc, x_ref, y_ref, f_ref,
                  transit, w_ref, send_sem, recv_sem, local_sem):
    row, col = lax.axis_index("row"), lax.axis_index("col")
    row_d, col_d = flip(row, (1, 2, 4)), flip(col, (1, 2, 4, 8))
    peers = [
        {"row": flipped(row, row_d, (1, 2, 4), dr), "col": flipped(col, col_d, (1, 2, 4, 8), dc)}
        for dr, dc in TARGETS
    ]
    barrier = pltpu.get_barrier_semaphore()
    for peer in peers:
        pl.semaphore_signal(barrier, inc=1, device_id=peer, device_id_type=MESH)

    high = row // 4
    code = row * 2 + high
    code_d = flip(code, (1, 2, 4, 8))

    def lanes(j):
        return pl.ds(pl.multiple_of((j % PER) * KC, KC), KC)

    def place(kind, mark, j):
        if kind == 2:
            return transit.at[j, mark]
        slot = flipped(code, code_d, (1, 2, 4, 8), mark)
        if kind == 0:
            return x_ref.at[j // PER, pl.ds(pl.multiple_of(slot * OWN, OWN), OWN), lanes(j)]
        slot = slot % 8
        return y_ref.at[j // PER, pl.ds(pl.multiple_of(slot * OWN, OWN), OWN), lanes(j)]

    for k in range(NK):
        x_ref[k, pl.ds(pl.multiple_of(col * OWN, OWN), OWN), :] = own_ref[pl.ds(k * KK, KK), :].T
    for t in range(NT_PTS):
        f_ref[t, :] = weights[t] * jnp.exp(-points[t] * den_ref[...])
    pl.semaphore_wait(barrier, len(TARGETS))

    k_col = col // 2
    bits = [((row // b) % 2 + (k_col // b) % 2) % 2 for b in (4, 2, 1)]
    which = (bits[0] * 4 + bits[1] * 2 + bits[2]) * 2 + ((col % 2) + high) % 2

    def arrived(kind, mark, event, j):
        ref = place(kind, mark, j)
        pltpu.make_async_copy(ref, ref, recv_sem.at[j, event]).wait()

    def act(action, j):
        _, _, event, kind, mark, kids, local = action
        if event >= 0:
            arrived(kind, mark, event, j)
        src = place(kind, mark, j)
        for target, to_kind, to_mark, to_event in kids:
            pltpu.make_async_remote_copy(
                src_ref=src, dst_ref=place(to_kind, to_mark, j),
                send_sem=send_sem.at[j], recv_sem=recv_sem.at[j, to_event],
                device_id=peers[target], device_id_type=MESH,
            ).start()
        if local:
            pltpu.make_async_copy(src, place(1, mark, j), local_sem.at[j]).start()

    def bulk_wait(sem, copies):
        ref = acc.at[0, pl.ds(0, copies * OWN * KC // (2 * COLS)), :]
        pltpu.make_async_copy(ref, ref, sem).wait()

    def choose(run, low, high):
        if high - low == 1:
            run(low)
            return
        middle = (low + high) // 2
        pl.when(which < middle)(lambda: choose(run, low, middle))
        pl.when(which >= middle)(lambda: choose(run, middle, high))

    def settle(j):
        def run(g):
            actions, last = PROGRAMS[g]
            for event, kind, mark in last:
                arrived(kind, mark, event, j)
            copies = sum(a[6] for a in actions)
            if copies:
                bulk_wait(local_sem.at[j], copies)

        choose(run, 0, len(PROGRAMS))

    def block(k, m):
        rows = pl.ds(pl.multiple_of(m * MB, MB), MB)
        weigh(x_ref[k, rows, :], lambda t: f_ref[pl.ds(t, 1), pl.ds(pl.multiple_of(k * KK, KK), KK)], w_ref)

        @pl.loop(0, COLS // NB)
        def _(n):
            at = pl.ds(pl.multiple_of(n * NB, NB), NB)
            for t in range(NT_PTS):
                acc[t, rows, at] += product(w_ref[pl.ds(t * MB, MB), :], y_ref[k, at, :])

    @pl.loop(0, STEPS)
    def _(p):
        k = jnp.maximum(p - START, 0) // PER
        part = jnp.maximum(p - START, 0) % PER
        busy = jnp.logical_and(p >= START, p < START + EARLY * PER)

        @pl.loop(0, NG)
        def _(group):
            def run(g):
                for at in range(NG):
                    mine = [a for a in PROGRAMS[g][0] if a[1] == at]

                    def go(mine=mine):
                        for lag, same in itertools.groupby(mine, lambda a: a[0]):
                            @pl.when(jnp.logical_and(p >= lag, p < NC + lag))
                            def _(lag=lag, same=tuple(same)):
                                for a in same:
                                    act(a, p - lag)
                    if NG > 1:
                        pl.when(group == at)(go)
                    else:
                        go()

            choose(run, 0, len(PROGRAMS))

            @pl.when(jnp.logical_and(busy, part == 0))
            def _():
                for i in range(PER):
                    settle(k * PER + i)

            if not EARLY:
                return

            @pl.when(jnp.logical_and(p == 0, group == 0))
            def _():
                @pl.loop(0, ROWS // 64)
                def _(m):
                    at = pl.ds(pl.multiple_of(m * 64, 64), 64)
                    acc[:, at, :] = jnp.zeros((NT_PTS, 64, COLS), F32)

            @pl.when(busy)
            def _():
                for b in range(NM // PER // NG):
                    block(k, (part * NG + group) * (NM // PER // NG) + b)

    @pl.loop(NC - PER * LAST, NC)
    def _(j):
        settle(j)

    def sent(g):
        @pl.loop(0, NC)
        def _(j):
            bulk_wait(send_sem.at[j], sum(len(a[5]) for a in PROGRAMS[g][0]))

    choose(sent, 0, len(PROGRAMS))


def last_kernel(acc, x_ref, y_ref, f_ref, out, w_ref, buf, sem):
    def copy(m, slot):
        return pltpu.make_async_copy(
            buf.at[slot], out.at[:, pl.ds(pl.multiple_of(m * MB2, MB2), MB2), :], sem.at[slot]
        )

    @pl.loop(0, NM2)
    def _(m):
        slot = m % 2
        rows = pl.ds(pl.multiple_of(m * MB2, MB2), MB2)

        @pl.when(m >= 2)
        def _():
            copy(m - 2, slot).wait()

        for k in range(EARLY, NK):
            at = slice(k * KK, (k + 1) * KK)
            weigh(x_ref[k, rows, :], lambda t: f_ref[t:t + 1, at], w_ref)
            for t in range(NT_PTS):
                d = product(w_ref[pl.ds(t * MB2, MB2), :], y_ref[k])
                if k > EARLY:
                    d += buf[slot, t]
                elif EARLY:
                    d += acc[t, rows, :]
                buf[slot, t] = d
        copy(m, slot).start()

    copy(NM2 - 2, (NM2 - 2) % 2).wait()
    copy(NM2 - 1, (NM2 - 1) % 2).wait()


def on_device(pair_ints, denominators, lap_points, lap_weights):
    vmem = pl.BlockSpec(memory_space=pltpu.VMEM)
    smem = pl.BlockSpec(memory_space=pltpu.SMEM)
    held = pl.pallas_call(
        gather_kernel,
        out_shape=(
            pltpu.VMEM((NT_PTS, ROWS, COLS), F32),
            pltpu.VMEM((NK, ROWS, KK), BF16),
            pltpu.VMEM((NK, COLS, KK), BF16),
            pltpu.VMEM((NT_PTS, PAIRS), F32),
        ),
        in_specs=[smem, smem, vmem, vmem],
        out_specs=(vmem,) * 4,
        scratch_shapes=[
            pltpu.VMEM((NC, NT, OWN, KC), BF16),
            pltpu.VMEM((NT_PTS * MB, KK), BF16),
            pltpu.SemaphoreType.DMA((NC,)),
            pltpu.SemaphoreType.DMA((NC, NE)),
            pltpu.SemaphoreType.DMA((NC,)),
        ],
        compiler_params=pltpu.CompilerParams(
            collective_id=0, has_side_effects=True, vmem_limit_bytes=VMEM_LIMIT
        ),
    )(lap_points, lap_weights, pair_ints, denominators)
    held = [pltpu.with_memory_space_constraint(a, pltpu.VMEM) for a in held]
    return pl.pallas_call(
        last_kernel,
        out_shape=jax.ShapeDtypeStruct((NT_PTS, ROWS, COLS), F32),
        in_specs=[vmem] * 4,
        out_specs=pl.BlockSpec(memory_space=pl.ANY),
        scratch_shapes=[
            pltpu.VMEM((NT_PTS * MB2, KK), BF16),
            pltpu.VMEM((2, NT_PTS, MB2, COLS), F32),
            pltpu.SemaphoreType.DMA((2,)),
        ],
        compiler_params=pltpu.CompilerParams(vmem_limit_bytes=VMEM_LIMIT),
    )(*held)


def solution(mesh):
    in_specs = (P(None, ("row", "col")), P(), P(), P())
    out_specs = P(None, "row", "col")
    return jax.shard_map(
        on_device, mesh=mesh, in_specs=in_specs, out_specs=out_specs, check_vma=False
    )
```
